512 devices in a mesh: pos: 16 (over z_lo, x), slab: 32 (over z_hi, y, core).
Axes of the slice: x: 4, y: 4, z: 16 (z_hi: 4, z_lo: 4; z = z_hi * 4 + z_lo), core: 2. Of those that a mesh axis runs over, the one named last changes fastest.
Arguments:
- labels: int32 [64, 256, 256], P('slab'), may hold values from 0 to 3
- magnet_mask: int32 [64, 256, 256], P('slab'), may hold values 0 or 1
- reluctivity: float32 [4], replicated, may hold values from 0.3 to 3
- rotor_shift: int32 [16], P('pos'), may hold values from 0 to 255
- potential: float32 [16, 64, 256, 256], P('pos', 'slab'), may hold values from -6 to 6
- adjoint_load: float32 [16, 64, 256, 256], P('pos', 'slab'), may hold values from -40 to 40
Outputs:
- shape_gradient: float32 [64, 256, 256], P('slab')
- adjoint: float32 [16, 64, 256, 256], P('pos', 'slab')
The draws below stay inside these ranges and needn't reach their ends.
All inputs are finite; a program needn't handle non-finite values. No bound on the sum of `magnet_mask` on one device may be relied on, other than what follows from the above.
Results may differ from the reference program's by a relative error of at most 0.0003.
Values sent between devices are 32-bit elements; how exact they have to be, the bound alone decides.
A program may use at most 64 MiB of HBM per device.

```python
import math
import jax
import jax.numpy as jnp

CX = 256
CY = 256
ITERS = 2
MATERIALS = 4
NZ = 64
N_POS = 16


def draw_adjoint_load(key, part):
    first_key = jax.random.fold_in(jax.random.fold_in(key, 11), 0)
    base = jax.random.truncated_normal(first_key, -4.0, 4.0, (N_POS, NZ, CX, CY), jnp.float32)
    depth = jnp.arange(NZ, dtype=jnp.float32) / max(NZ - 1, 1)
    rising = jnp.exp(jnp.log(3.0) * depth)[None, :, None, None]
    return base * rising


def with_ends(drawn, stream_key, least, high):
    spot = [jax.random.randint(jax.random.fold_in(stream_key, axis), (), 0, length) for axis, length in enumerate(drawn.shape)]
    widest = drawn.shape.index(max(drawn.shape))
    neighbour = spot[:widest] + [(spot[widest] + 1) % drawn.shape[widest]] + spot[widest + 1:]
    return drawn.at[tuple(spot)].set(least).at[tuple(neighbour)].set(high)


def block_levels(own_key, extent, cuts, smallest, high):
    loudness = 1.0
    for axis_at, blocks in cuts:
        heights = jax.random.uniform(jax.random.fold_in(jax.random.fold_in(own_key, 6), axis_at), (blocks,), jnp.float32, smallest / len(cuts), high / len(cuts))
        loudness = loudness * jnp.repeat(jnp.exp(heights), extent[axis_at] // blocks).reshape((-1,) + (1,) * (len(extent) - 1 - axis_at))
    return loudness


def scatter_about(key, extent, width, limit, pieces=(), held_as=jnp.bfloat16):
    loudness = block_levels(key, extent, pieces, -0.22, 0.18) if pieces else 1.0
    values = jax.random.normal(key, extent, jnp.float32) * width * loudness
    return jnp.minimum(jnp.maximum(values, -limit), limit).astype(held_as)


def setup_inputs(seed: int = 0) -> dict:
    key_list = jax.random.split(jax.random.key(seed), 7)
    return {
        "labels": with_ends(jax.random.randint(key_list[0], (NZ, CX, CY), 0, 4), jax.random.fold_in(key_list[0], 1), 0, 3).astype(jnp.int32),
        "magnet_mask": with_ends((jax.random.randint(key_list[1], (NZ, CX, CY), 0, 2) < 1).astype(jnp.int32), jax.random.fold_in(key_list[1], 1), 0, 1),
        "reluctivity": jnp.clip(jnp.exp(jax.random.uniform(key_list[2], (MATERIALS,), jnp.float32, math.log(0.3), math.log(3.0))), 0.3, 3.0),
        "rotor_shift": with_ends(jax.random.randint(key_list[3], (N_POS,), 0, CY), jax.random.fold_in(key_list[3], 1), 0, CY - 1).astype(jnp.int32),
        "potential": scatter_about(key_list[4], (N_POS, NZ, CX, CY), 1.0, 6.0, ((0, 16), (1, 32)), jnp.float32),
        "adjoint_load": draw_adjoint_load(jax.random.fold_in(key_list[6], 71), 0),
    }


diagonal_shift = 0.5


def material_field(labels, reluctivity, offset):
    rotated = jnp.roll(labels, offset, axis=2)
    radial = jax.lax.broadcasted_iota(jnp.int32, labels.shape, 1)
    material = jnp.where(radial < labels.shape[1] // 2, rotated, labels)
    result = jnp.zeros(labels.shape, jnp.float32)
    for index in range(4):
        result = result + (material == index).astype(jnp.float32) * reluctivity[index]
    return result


def apply_operator(field, padded_field, relief, padded_relief):
    result = diagonal_shift * field
    result = result + 0.5 * (relief + padded_relief[2:]) * (field - padded_field[2:])
    result = result + 0.5 * (relief + padded_relief[:-2]) * (field - padded_field[:-2])
    radial_field = jnp.pad(field, ((0, 0), (1, 1), (0, 0)))
    radial_relief = jnp.pad(relief, ((0, 0), (1, 1), (0, 0)))
    result = result + 0.5 * (relief + radial_relief[:, 2:]) * (field - radial_field[:, 2:])
    result = result + 0.5 * (relief + radial_relief[:, :-2]) * (field - radial_field[:, :-2])
    for offset in (1, -1):
        result = result + 0.5 * (relief + jnp.roll(relief, offset, 2)) * (field - jnp.roll(field, offset, 2))
    return result


def gradient_term(stacked, padded_stack, relief, magnet_mask):
    axial = 0.5 * (padded_stack[:, 2:] - padded_stack[:, :-2])
    radial_pad = jnp.pad(stacked, ((0, 0), (0, 0), (1, 1), (0, 0)))
    radial = 0.5 * (radial_pad[:, :, 2:] - radial_pad[:, :, :-2])
    angular = 0.5 * (jnp.roll(stacked, -1, 3) - jnp.roll(stacked, 1, 3))
    inner = axial[0] * axial[1] + radial[0] * radial[1] + angular[0] * angular[1]
    square = axial[0] * axial[0] + radial[0] * radial[0] + angular[0] * angular[0]
    return magnet_mask.astype(jnp.float32) * relief * (inner + 0.5 * square)


def reference(labels, magnet_mask, reluctivity, rotor_shift, potential, adjoint_load):
    summed = jnp.zeros(labels.shape, jnp.float32)
    adjoints = []
    for position in range(N_POS):
        relief = material_field(labels, reluctivity, rotor_shift[position])
        padded_relief = jnp.pad(relief, ((1, 1), (0, 0), (0, 0)))

        def operate(field):
            return apply_operator(field, jnp.pad(field, ((1, 1), (0, 0), (0, 0))), relief, padded_relief)

        solution = jnp.zeros(relief.shape, jnp.float32)
        residual = adjoint_load[position]
        direction = residual
        norm_now = jnp.sum(residual * residual)
        for iteration in range(ITERS):
            image = operate(direction)
            alpha = norm_now / jnp.sum(direction * image)
            solution = solution + alpha * direction
            residual = residual - alpha * image
            norm_next = jnp.sum(residual * residual)
            direction = residual + (norm_next / norm_now) * direction
            norm_now = norm_next
        adjoints.append(solution)
        stacked = jnp.stack([potential[position], solution])
        padded_stack = jnp.pad(stacked, ((0, 0), (1, 1), (0, 0), (0, 0)))
        summed = summed + gradient_term(stacked, padded_stack, relief, magnet_mask)
    return summed / N_POS, jnp.stack(adjoints)
```

```python
import jax
import jax.numpy as jnp
from jax import lax
from jax.experimental import pallas as pl
from jax.experimental.pallas import tpu as pltpu
from jax.sharding import PartitionSpec as P

MESH = pl.DeviceIdType.MESH
PAD = 8
ROWS = 32
diagonal_shift = 0.5


def fold(block):
    half = block.shape[1] // 2
    narrow = block[:, :half] + block[:, half:]
    return narrow.reshape(narrow.shape[0] // 8, 8, half).sum(axis=0)


def kernel(
    reluctivity, shift, labels, mask, potential, load, gradient, adjoint,
    label_x, nu_x, d_x, w_x, r_x, a_x, pot_x, mask_x, term, tile, near, far,
    part_x, part_z, piece, merged, local_sem, send_sem, recv_sem,
    near_send, near_recv, far_send, far_recv, x_send, x_recv, z_send, z_recv, out_sem,
):
    pos, slab = lax.axis_index("pos"), lax.axis_index("slab")
    n_slab = lax.axis_size("slab")
    up, down = lax.rem(slab + 1, n_slab), lax.rem(slab + n_slab - 1, n_slab)
    z_hi, inner = slab // 8, lax.rem(slab, 8)
    z_lo, x = pos // 4, lax.rem(pos, 4)
    cx, cy = labels.shape[1], labels.shape[2]

    local = [
        pltpu.make_async_copy(source, target, local_sem.at[i])
        for i, (source, target) in enumerate(
            (
                (load.at[0], d_x.at[pl.ds(1, 2), pl.ds(PAD, cx)]),
                (labels, label_x.at[pl.ds(1, 2)]),
                (potential.at[0], pot_x.at[pl.ds(1, 2), pl.ds(PAD, cx)]),
                (mask, mask_x),
            )
        )
    ]
    for copy in local:
        copy.start()

    def near_peer(o):
        return {"slab": z_hi * 8 + lax.rem(inner + o, 8)}

    def far_peer(o):
        return {"slab": lax.rem(z_hi + o, 4) * 8 + inner}

    def x_index(o):
        return lax.rem(x + o, 4)

    def z_index(o):
        return lax.rem(z_lo + o, 4)

    peers = [{"slab": up}, {"slab": down}]
    peers += [near_peer(o) for o in range(1, 8)]
    peers += [far_peer(o) for o in range(1, 4)]
    peers += [{"pos": z_lo * 4 + x_index(o)} for o in range(1, 4)]
    peers += [{"pos": z_index(o) * 4 + x} for o in range(1, 4)]
    barrier = pltpu.get_barrier_semaphore()
    for peer in peers:
        pl.semaphore_signal(barrier, inc=1, device_id=peer, device_id_type=MESH)
    pl.semaphore_wait(barrier, len(peers))

    def halo(which, first, last, target):
        return [
            pltpu.make_async_remote_copy(
                src_ref=source,
                dst_ref=target(ghost),
                send_sem=send_sem.at[2 * which + side],
                recv_sem=recv_sem.at[2 * which + side],
                device_id={"slab": peer},
                device_id_type=MESH,
            )
            for side, (source, ghost, peer) in enumerate(((last, 0, up), (first, 3, down)))
        ]

    def padded(ref):
        return lambda layer: ref.at[layer, pl.ds(PAD, cx)]

    d_halo = halo(0, load.at[0, 0], load.at[0, 1], padded(d_x))
    label_halo = halo(1, labels.at[0], labels.at[1], lambda layer: label_x.at[layer])
    pot_halo = halo(2, potential.at[0, 0], potential.at[0, 1], padded(pot_x))
    for copy in d_halo + label_halo + pot_halo:
        copy.start()

    for ref in (nu_x, d_x, r_x, a_x, pot_x):
        for layer in (1, 2):
            ref[layer, pl.ds(0, PAD), :] = jnp.zeros((PAD, cy), jnp.float32)
            ref[layer, pl.ds(PAD + cx, PAD), :] = jnp.zeros((PAD, cy), jnp.float32)

    low = jnp.where(slab > 0, 1.0, 0.0)
    high = jnp.where(slab < n_slab - 1, 1.0, 0.0)
    live = (low, 1.0, 1.0, high)
    table = [reluctivity[i] for i in range(4)]
    offset = shift[0]

    def materials(layers):
        def lookup(index):
            result = jnp.where(index == 1, table[1], table[0])
            result = jnp.where(index == 2, table[2], result)
            return jnp.where(index == 3, table[3], result)

        @pl.loop(0, cx // 2 // ROWS)
        def _(i):
            r = pl.multiple_of(i * ROWS, ROWS)
            s = pl.multiple_of(i * ROWS + cx // 2, ROWS)
            for layer in layers:
                turned = pltpu.roll(lookup(label_x[layer, pl.ds(r, ROWS), :]), offset, 1)
                nu_x[layer, pl.ds(PAD + r, ROWS), :] = turned * live[layer]
                still = lookup(label_x[layer, pl.ds(s, ROWS), :])
                nu_x[layer, pl.ds(PAD + s, ROWS), :] = still * live[layer]

    def at(ref, layer, r):
        return ref[layer, pl.ds(PAD + r, ROWS), :]

    def tall(ref, layer, r):
        return ref[layer, pl.ds(r, ROWS + 2 * PAD), :]

    def middle(block):
        return block[PAD : PAD + ROWS]

    def before(block):
        return pltpu.roll(block, 1, 0)

    def after(block):
        return pltpu.roll(block, ROWS + 2 * PAD - 1, 0)

    def operator(ref, layer, r, below, above):
        v_tall, nu_tall = tall(ref, layer, r), tall(nu_x, layer, r)
        flux = 0.5 * (nu_tall + after(nu_tall)) * (v_tall - after(v_tall))
        v, nu = middle(v_tall), middle(nu_tall)
        result = diagonal_shift * v + middle(flux - before(flux))
        for other_nu, other in ((at(nu_x, layer - 1, r), below), (at(nu_x, layer + 1, r), above)):
            result += 0.5 * (nu + other_nu) * (v - other)
        flux = 0.5 * (nu + pltpu.roll(nu, cy - 1, 1)) * (v - pltpu.roll(v, cy - 1, 1))
        return v, result + (flux - pltpu.roll(flux, 1, 1))

    zero = jnp.zeros((8, cy // 2), jnp.float32)

    local[1].wait()
    materials((1, 2))
    for copy in label_halo:
        copy.wait()
    materials((0, 3))
    local[0].wait()
    for copy in d_halo:
        copy.wait()

    def first_pass(i, sums):
        norm, energy = sums
        r = pl.multiple_of(i * ROWS, ROWS)
        edge = (at(d_x, 0, r) * low, at(d_x, 3, r) * high)
        for layer in (1, 2):
            below = edge[0] if layer == 1 else at(d_x, 1, r)
            above = edge[1] if layer == 2 else at(d_x, 2, r)
            v, image = operator(d_x, layer, r, below, above)
            w_x[layer, pl.ds(r, ROWS), :] = image
            norm += fold(v * v)
            energy += fold(v * image)
        return norm, energy

    sums = lax.fori_loop(0, cx // ROWS, first_pass, (zero, zero))

    w_halo = halo(3, w_x.at[1], w_x.at[2], lambda layer: w_x.at[layer])
    for copy in w_halo:
        copy.start()

    def reduce(which, parts):
        for i, part in enumerate(parts):
            tile[which, 0, pl.ds(i, 1), :] = jnp.sum(part, axis=0, keepdims=True)

        def exchange(stage, size, mine, box, peer, send, recv):
            copies = [
                pltpu.make_async_remote_copy(
                    src_ref=tile.at[which, stage],
                    dst_ref=box.at[which, mine],
                    send_sem=send.at[which, o - 1],
                    recv_sem=recv.at[which, o - 1],
                    device_id=peer(o),
                    device_id_type=MESH,
                )
                for o in range(1, size)
            ]
            for copy in copies:
                copy.start()
            box[which, mine] = tile[which, stage]
            for copy in copies:
                copy.wait()
            return sum((box[which, i] for i in range(1, size)), box[which, 0])

        tile[which, 1] = exchange(0, 8, inner, near, near_peer, near_send, near_recv)
        total = exchange(1, 4, z_hi, far, far_peer, far_send, far_recv)
        return [jnp.sum(total[i : i + 1, :], axis=1, keepdims=True) for i in range(len(parts))]

    rr0, energy0 = reduce(0, sums)
    alpha0 = rr0 / energy0
    for copy in w_halo:
        copy.wait()

    @pl.loop(0, cx // ROWS)
    def _(i):
        r = pl.multiple_of(i * ROWS, ROWS)
        for layer in range(4):
            rest = at(d_x, layer, r) - alpha0 * w_x[layer, pl.ds(r, ROWS), :]
            r_x[layer, pl.ds(PAD + r, ROWS), :] = rest * live[layer]

    def second_pass(i, sums):
        norm, energy, cross = sums
        r = pl.multiple_of(i * ROWS, ROWS)
        for layer in (1, 2):
            v, image = operator(r_x, layer, r, at(r_x, layer - 1, r), at(r_x, layer + 1, r))
            norm += fold(v * v)
            energy += fold(v * image)
            cross += fold(v * w_x[layer, pl.ds(r, ROWS), :])
        return norm, energy, cross

    sums = lax.fori_loop(0, cx // ROWS, second_pass, (zero, zero, zero))
    rr1, energy1, cross1 = reduce(1, sums)
    beta = rr1 / rr0
    alpha1 = rr1 / (energy1 + beta * (2.0 * cross1 + beta * energy0))
    scale = alpha0 + alpha1 * beta

    @pl.loop(0, cx // ROWS)
    def _(i):
        r = pl.multiple_of(i * ROWS, ROWS)
        for layer in range(4):
            value = scale * (at(d_x, layer, r) * live[layer]) + alpha1 * at(r_x, layer, r)
            a_x[layer, pl.ds(PAD + r, ROWS), :] = value

    finish = pltpu.make_async_copy(a_x.at[pl.ds(1, 2), pl.ds(PAD, cx)], adjoint.at[0], out_sem.at[0])
    finish.start()
    local[2].wait()
    local[3].wait()
    for copy in pot_halo:
        copy.wait()

    def slopes(ref, layer, r, below, above):
        v_tall = tall(ref, layer, r)
        v = middle(v_tall)
        return (
            above - below,
            middle(after(v_tall) - before(v_tall)),
            pltpu.roll(v, cy - 1, 1) - pltpu.roll(v, 1, 1),
        )

    @pl.loop(0, cx // ROWS)
    def _(i):
        r = pl.multiple_of(i * ROWS, ROWS)
        for layer in (1, 2):
            below, above = at(pot_x, layer - 1, r), at(pot_x, layer + 1, r)
            if layer == 1:
                below = below * low
            else:
                above = above * high
            pot = slopes(pot_x, layer, r, below, above)
            adj = slopes(a_x, layer, r, at(a_x, layer - 1, r), at(a_x, layer + 1, r))
            total = sum(p * (a + 0.5 * p) for p, a in zip(pot, adj))
            chosen = mask_x[layer - 1, pl.ds(r, ROWS), :].astype(jnp.float32)
            value = 0.25 * chosen * at(nu_x, layer, r) * total
            term[pl.ds((layer - 1) * cx + r, ROWS), :] = value

    quarter, small = 2 * cx // 4, 2 * cx // 16

    def scatter(mine, index, peer, source, size, box, send, recv):
        return [
            pltpu.make_async_remote_copy(
                src_ref=source.at[pl.ds(pl.multiple_of(index(o) * size, size), size)],
                dst_ref=box.at[o - 1],
                send_sem=send.at[0, o - 1],
                recv_sem=recv.at[0, o - 1],
                device_id=peer(o),
                device_id_type=MESH,
            )
            for o in range(1, 4)
        ]

    def x_peer(o):
        return {"pos": z_lo * 4 + x_index(o)}

    def z_peer(o):
        return {"pos": z_index(o) * 4 + x}

    copies = scatter(x, x_index, x_peer, term, quarter, part_x, x_send, x_recv)
    for copy in copies:
        copy.start()
    for copy in copies:
        copy.wait()

    @pl.loop(0, quarter // ROWS)
    def _(i):
        r = pl.multiple_of(i * ROWS, ROWS)
        own = term[pl.ds(pl.multiple_of(x * quarter + r, ROWS), ROWS), :]
        for o in range(3):
            own += part_x[o, pl.ds(r, ROWS), :]
        piece[pl.ds(r, ROWS), :] = own

    copies = scatter(z_lo, z_index, z_peer, piece, small, part_z, z_send, z_recv)
    for copy in copies:
        copy.start()
    for copy in copies:
        copy.wait()

    own_small = pl.ds(pl.multiple_of(x * quarter + z_lo * small, small), small)
    total = piece[pl.ds(pl.multiple_of(z_lo * small, small), small), :]
    for o in range(3):
        total += part_z[o]
    merged[own_small, :] = total / lax.axis_size("pos")

    def spread(where, peer, send, recv):
        return [
            pltpu.make_async_remote_copy(
                src_ref=merged.at[where],
                dst_ref=merged.at[where],
                send_sem=send.at[1, o - 1],
                recv_sem=recv.at[1, o - 1],
                device_id=peer(o),
                device_id_type=MESH,
            )
            for o in range(1, 4)
        ]

    copies = spread(own_small, z_peer, z_send, z_recv)
    for copy in copies:
        copy.start()
    for copy in copies:
        copy.wait()
    own_quarter = pl.ds(pl.multiple_of(x * quarter, quarter), quarter)
    copies = spread(own_quarter, x_peer, x_send, x_recv)
    for copy in copies:
        copy.start()
    for copy in copies:
        copy.wait()
    outs = [
        pltpu.make_async_copy(merged.at[pl.ds(layer * cx, cx)], gradient.at[layer], out_sem.at[1 + layer])
        for layer in range(2)
    ]
    for copy in outs:
        copy.start()
    for copy in outs:
        copy.wait()
    finish.wait()


def local(labels, magnet_mask, reluctivity, rotor_shift, potential, adjoint_load):
    cx, cy = labels.shape[1:]
    tall = cx + 2 * PAD
    floats = lambda *shape: pltpu.VMEM(shape, jnp.float32)
    sems = pltpu.SemaphoreType.DMA
    return pl.pallas_call(
        kernel,
        out_shape=(
            jax.ShapeDtypeStruct(labels.shape, jnp.float32),
            jax.ShapeDtypeStruct(adjoint_load.shape, jnp.float32),
        ),
        in_specs=[pl.BlockSpec(memory_space=pltpu.SMEM)] * 2 + [pl.BlockSpec(memory_space=pl.ANY)] * 4,
        out_specs=(pl.BlockSpec(memory_space=pl.ANY),) * 2,
        scratch_shapes=[
            pltpu.VMEM((4, cx, cy), jnp.int32),
            floats(4, tall, cy),
            floats(4, tall, cy),
            floats(4, cx, cy),
            floats(4, tall, cy),
            floats(4, tall, cy),
            floats(4, tall, cy),
            pltpu.VMEM((2, cx, cy), jnp.int32),
            floats(2 * cx, cy),
            floats(2, 2, 8, 128),
            floats(2, 8, 8, 128),
            floats(2, 4, 8, 128),
            floats(3, cx // 2, cy),
            floats(3, cx // 8, cy),
            floats(cx // 2, cy),
            floats(2 * cx, cy),
            sems((4,)),
            sems((8,)),
            sems((8,)),
            sems((2, 7)),
            sems((2, 7)),
            sems((2, 3)),
            sems((2, 3)),
            sems((2, 3)),
            sems((2, 3)),
            sems((2, 3)),
            sems((2, 3)),
            sems((3,)),
        ],
        compiler_params=pltpu.CompilerParams(
            collective_id=0, has_side_effects=True, vmem_limit_bytes=32 << 20
        ),
    )(reluctivity, rotor_shift, labels, magnet_mask, potential, adjoint_load)


def solution(mesh):
    return jax.shard_map(
        local,
        mesh=mesh,
        in_specs=(
            P("slab", None, None),
            P("slab", None, None),
            P(),
            P("pos"),
            P("pos", "slab", None, None),
            P("pos", "slab", None, None),
        ),
        out_specs=(P("slab", None, None), P("pos", "slab", None, None)),
        check_vma=False,
    )
```

```python
import jax
import jax.numpy as jnp
from jax import lax
from jax.experimental import pallas as pl
from jax.experimental.pallas import tpu as pltpu
from jax.sharding import PartitionSpec as P

MESH = pl.DeviceIdType.MESH
PAD = 8
ROWS = 32
diagonal_shift = 0.5


def fold(block):
    half = block.shape[1] // 2
    narrow = block[:, :half] + block[:, half:]
    return narrow.reshape(narrow.shape[0] // 8, 8, half).sum(axis=0)


def kernel(
    reluctivity, shift, labels, mask, potential, load, gradient, adjoint,
    label_x, nu_x, d_x, w_x, a_x, pot_x, mask_x, term, relay, relay_label, tile, near, far,
    part_x, part_z, piece, merged, local_sem, send_sem, recv_sem, relay_send, relay_recv,
    near_send, near_recv, far_send, far_recv, x_send, x_recv, z_send, z_recv, out_sem,
):
    pos, slab = lax.axis_index("pos"), lax.axis_index("slab")
    n_slab = lax.axis_size("slab")
    up, down = lax.rem(slab + 1, n_slab), lax.rem(slab + n_slab - 1, n_slab)
    z_hi, inner = slab // 8, lax.rem(slab, 8)
    z_lo, x = pos // 4, lax.rem(pos, 4)
    cx, cy = labels.shape[1], labels.shape[2]

    local = [
        pltpu.make_async_copy(source, target, local_sem.at[i])
        for i, (source, target) in enumerate(
            (
                (load.at[0], d_x.at[pl.ds(1, 2), pl.ds(PAD, cx)]),
                (labels, label_x.at[pl.ds(1, 2)]),
                (potential.at[0], pot_x.at[pl.ds(1, 2), pl.ds(PAD, cx)]),
                (mask, mask_x),
            )
        )
    ]
    for copy in local:
        copy.start()

    def near_peer(o):
        return {"slab": z_hi * 8 + lax.rem(inner + o, 8)}

    def far_peer(o):
        return {"slab": lax.rem(z_hi + o, 4) * 8 + inner}

    def x_index(o):
        return lax.rem(x + o, 4)

    def z_index(o):
        return lax.rem(z_lo + o, 4)

    peers = [{"slab": up}, {"slab": down}]
    peers += [near_peer(o) for o in range(1, 8)]
    peers += [far_peer(o) for o in range(1, 4)]
    peers += [{"pos": z_lo * 4 + x_index(o)} for o in range(1, 4)]
    peers += [{"pos": z_index(o) * 4 + x} for o in range(1, 4)]
    barrier = pltpu.get_barrier_semaphore()

    def greet(peer):
        pl.semaphore_signal(barrier, inc=1, device_id=peer, device_id_type=MESH)

    z_up, z_down = lax.rem(z_hi + 1, 4) * 8, lax.rem(z_hi + 3, 4) * 8
    is_first, is_last = inner == 0, inner == 7
    odd = lax.rem(inner, 2) == 1
    is_up_relay = jnp.logical_and(odd, inner < 7)
    is_down_relay = jnp.logical_and(jnp.logical_not(odd), inner > 0)
    for peer in peers:
        greet(peer)

    @pl.when(is_first)
    def _():
        for i in (1, 3, 5):
            greet({"slab": z_down + i})

    @pl.when(is_last)
    def _():
        for i in (2, 4, 6):
            greet({"slab": z_up + i})

    @pl.when(is_up_relay)
    def _():
        greet({"slab": z_up})

    @pl.when(is_down_relay)
    def _():
        greet({"slab": z_down + 7})

    ends = jnp.logical_or(is_first, is_last)
    pl.semaphore_wait(barrier, len(peers) + jnp.where(ends, 3, 1))
    strip = cx // 4
    row = inner // 2

    class Halo:
        def __init__(self, which, first, last, target, buffer):
            def send(source, where, peer, side, k):
                return pltpu.make_async_remote_copy(
                    src_ref=source,
                    dst_ref=where,
                    send_sem=send_sem.at[which, side, k],
                    recv_sem=recv_sem.at[which, side, k],
                    device_id={"slab": peer},
                    device_id_type=MESH,
                )

            def through(source, k, peer):
                return pltpu.make_async_remote_copy(
                    src_ref=source.at[pl.ds(k * strip, strip)],
                    dst_ref=buffer,
                    send_sem=send_sem.at[which, 2, k],
                    recv_sem=relay_recv.at[which],
                    device_id={"slab": peer},
                    device_id_type=MESH,
                )

            def forward(side, ghost, peer):
                where = pl.ds(pl.multiple_of(row * strip, strip), strip)
                return pltpu.make_async_remote_copy(
                    src_ref=buffer,
                    dst_ref=target(ghost).at[where],
                    send_sem=relay_send.at[which],
                    recv_sem=recv_sem.at[which, side, row],
                    device_id={"slab": peer},
                    device_id_type=MESH,
                )

            def pieces(source, side, ghost, peer):
                return [
                    send(
                        source.at[pl.ds(k * strip, strip)],
                        target(ghost).at[pl.ds(k * strip, strip)],
                        peer, side, k,
                    )
                    for k in range(4)
                ]

            self.whole = [
                (send(last, target(0), up, 0, 0), is_last, is_first),
                (send(first, target(3), down, 1, 0), is_first, is_last),
            ]
            self.parts = [pieces(last, 0, 0, up), pieces(first, 1, 3, down)]
            self.through = [
                [through(last, k, z_hi * 8 + 2 * k + 1) for k in (0, 1, 2)],
                [through(first, k, z_hi * 8 + 2 * k) for k in (1, 2, 3)],
            ]
            self.forward = [
                (is_up_relay, forward(0, 0, z_up)),
                (is_down_relay, forward(1, 3, z_down + 7)),
            ]
            self.arrive = through(last, 0, z_hi * 8)

        def start(self):
            for side, (copy, leaves, _) in enumerate(self.whole):
                direct = self.parts[side][3 - 3 * side]

                @pl.when(leaves)
                def _():
                    for piece in self.through[side]:
                        piece.start()
                    direct.start()

                @pl.when(jnp.logical_not(leaves))
                def _():
                    copy.start()

        def relay(self):
            for role, copy in self.forward:

                @pl.when(role)
                def _():
                    self.arrive.wait_recv()
                    copy.start()

        def wait(self):
            for side, (copy, leaves, enters) in enumerate(self.whole):
                direct = self.parts[side][3 - 3 * side]

                @pl.when(enters)
                def _():
                    for piece in self.parts[side]:
                        piece.wait_recv()

                @pl.when(jnp.logical_not(enters))
                def _():
                    copy.wait_recv()

                @pl.when(leaves)
                def _():
                    for piece in self.through[side]:
                        piece.wait_send()
                    direct.wait_send()

                @pl.when(jnp.logical_not(leaves))
                def _():
                    copy.wait_send()

            for role, copy in self.forward:

                @pl.when(role)
                def _():
                    copy.wait_send()

    def padded(ref):
        return lambda layer: ref.at[layer, pl.ds(PAD, cx)]

    d_halo = Halo(0, load.at[0, 0], load.at[0, 1], padded(d_x), relay.at[0])
    label_halo = Halo(1, labels.at[0], labels.at[1], lambda layer: label_x.at[layer], relay_label)
    pot_halo = Halo(2, potential.at[0, 0], potential.at[0, 1], padded(pot_x), relay.at[1])
    w_halo = Halo(3, padded(w_x)(1), padded(w_x)(2), padded(w_x), relay.at[2])
    label_halo.start()
    d_halo.start()

    for ref in (nu_x, d_x, w_x, a_x, pot_x):
        for layer in (1, 2):
            ref[layer, pl.ds(0, PAD), :] = jnp.zeros((PAD, cy), jnp.float32)
            ref[layer, pl.ds(PAD + cx, PAD), :] = jnp.zeros((PAD, cy), jnp.float32)

    low = jnp.where(slab > 0, 1.0, 0.0)
    high = jnp.where(slab < n_slab - 1, 1.0, 0.0)
    live = (low, 1.0, 1.0, high)
    table = [reluctivity[i] for i in range(4)]
    offset = shift[0]

    def materials(layers):
        def lookup(index):
            result = jnp.where(index == 1, table[1], table[0])
            result = jnp.where(index == 2, table[2], result)
            return jnp.where(index == 3, table[3], result)

        @pl.loop(0, cx // 2 // ROWS)
        def _(i):
            r = pl.multiple_of(i * ROWS, ROWS)
            s = pl.multiple_of(i * ROWS + cx // 2, ROWS)
            for layer in layers:
                turned = pltpu.roll(lookup(label_x[layer, pl.ds(r, ROWS), :]), offset, 1)
                nu_x[layer, pl.ds(PAD + r, ROWS), :] = turned * live[layer]
                still = lookup(label_x[layer, pl.ds(s, ROWS), :])
                nu_x[layer, pl.ds(PAD + s, ROWS), :] = still * live[layer]

    def at(ref, layer, r):
        return ref[layer, pl.ds(PAD + r, ROWS), :]

    def tall(ref, layer, r):
        return ref[layer, pl.ds(r, ROWS + 2 * PAD), :]

    def middle(block):
        return block[PAD : PAD + ROWS]

    def before(block):
        return pltpu.roll(block, 1, 0)

    def after(block):
        return pltpu.roll(block, ROWS + 2 * PAD - 1, 0)

    def operator(ref, layer, r, below, above):
        v_tall, nu_tall = tall(ref, layer, r), tall(nu_x, layer, r)
        flux = 0.5 * (nu_tall + after(nu_tall)) * (v_tall - after(v_tall))
        v, nu = middle(v_tall), middle(nu_tall)
        result = diagonal_shift * v + middle(flux - before(flux))
        for other_nu, other in ((at(nu_x, layer - 1, r), below), (at(nu_x, layer + 1, r), above)):
            result += 0.5 * (nu + other_nu) * (v - other)
        flux = 0.5 * (nu + pltpu.roll(nu, cy - 1, 1)) * (v - pltpu.roll(v, cy - 1, 1))
        return v, result + (flux - pltpu.roll(flux, 1, 1))

    zero = jnp.zeros((8, cy // 2), jnp.float32)

    local[1].wait()
    materials((1, 2))
    label_halo.relay()
    d_halo.relay()
    label_halo.wait()
    materials((0, 3))
    local[0].wait()
    d_halo.wait()

    def sides(ref, layer, r):
        below, above = at(ref, layer - 1, r), at(ref, layer + 1, r)
        return (below * low, above) if layer == 1 else (below, above * high)

    def first_pass(i, sums):
        norm, energy = sums
        r = pl.multiple_of(i * ROWS, ROWS)
        for layer in (1, 2):
            v, image = operator(d_x, layer, r, *sides(d_x, layer, r))
            w_x[layer, pl.ds(PAD + r, ROWS), :] = image
            norm += fold(v * v)
            energy += fold(v * image)
        return norm, energy

    sums = lax.fori_loop(0, cx // ROWS, first_pass, (zero, zero))
    w_halo.start()

    def whole_sum(part):
        return jnp.sum(jnp.sum(part, axis=0, keepdims=True), axis=1, keepdims=True)

    def wide(value, width=cy):
        return jnp.broadcast_to(value[:, :1], (1, width))

    def quotient(top, bottom):
        some = bottom > 0.0
        return jnp.where(some, top / jnp.where(some, bottom, 1.0), 0.0)

    norm, energy = [whole_sum(part) for part in sums]
    theta = quotient(energy, norm)
    theta_wide = wide(theta)
    w_halo.relay()
    w_halo.wait()
    pot_halo.start()

    def second_pass(i, sums):
        m1, m2, m3, m4 = sums
        r = pl.multiple_of(i * ROWS, ROWS)
        for layer in (1, 2):
            w, image = operator(w_x, layer, r, *sides(w_x, layer, r))
            d = at(d_x, layer, r)
            u = w - theta_wide * d
            q = image - theta_wide * w
            m1 += fold(d * u)
            m2 += fold(u * u)
            m3 += fold(u * q)
            m4 += fold(d * q)
        return m1, m2, m3, m4

    sums = lax.fori_loop(0, cx // ROWS, second_pass, (zero,) * 4)

    def combine(box):
        th, m0, m1, m2, m3, m4 = [box[:, i, :] for i in range(6)]
        total = lambda value: jnp.sum(value, axis=0, keepdims=True)
        centre = quotient(total(th * m0 + m1), total(m0))
        e = centre - th
        dw = m1 + th * m0
        return (
            centre,
            total(m0),
            total(m1 - e * m0),
            total(m2 - e * (2.0 * m1 - e * m0)),
            total(m3 - e * (m2 + th * m1 + m4 - e * dw)),
            total(m4 - e * dw),
        )

    def exchange(stage, values, size, mine, box, peer, send, recv):
        for i, value in enumerate(values):
            tile[stage, pl.ds(i, 1), :] = wide(value, tile.shape[2])
        copies = [
            pltpu.make_async_remote_copy(
                src_ref=tile.at[stage],
                dst_ref=box.at[mine],
                send_sem=send.at[o - 1],
                recv_sem=recv.at[o - 1],
                device_id=peer(o),
                device_id_type=MESH,
            )
            for o in range(1, size)
        ]
        for copy in copies:
            copy.start()
        box[mine] = tile[stage]
        for copy in copies:
            copy.wait()
        return combine(box)

    values = (theta, norm, *[whole_sum(part) for part in sums])
    values = exchange(0, values, 8, inner, near, near_peer, near_send, near_recv)
    pot_halo.relay()
    values = exchange(1, values, 4, z_hi, far, far_peer, far_send, far_recv)
    centre, m0, _, m2, m3, _ = values
    alpha0 = 1.0 / centre
    beta = alpha0 * alpha0 * m2 / m0
    alpha1 = m2 / (m3 - alpha0 * m2 * (m2 / m0))
    from_d = wide(alpha0 + alpha1 * (1.0 + beta))
    from_w = wide(alpha0 * alpha1)

    @pl.loop(0, cx // ROWS)
    def _(i):
        r = pl.multiple_of(i * ROWS, ROWS)
        for layer in range(4):
            value = from_d * at(d_x, layer, r) - from_w * at(w_x, layer, r)
            a_x[layer, pl.ds(PAD + r, ROWS), :] = value * live[layer]

    finish = pltpu.make_async_copy(a_x.at[pl.ds(1, 2), pl.ds(PAD, cx)], adjoint.at[0], out_sem.at[0])
    finish.start()
    local[2].wait()
    local[3].wait()
    pot_halo.wait()

    def slopes(ref, layer, r, below, above):
        v_tall = tall(ref, layer, r)
        v = middle(v_tall)
        return (
            above - below,
            middle(after(v_tall) - before(v_tall)),
            pltpu.roll(v, cy - 1, 1) - pltpu.roll(v, 1, 1),
        )

    @pl.loop(0, cx // ROWS)
    def _(i):
        r = pl.multiple_of(i * ROWS, ROWS)
        for layer in (1, 2):
            pot = slopes(pot_x, layer, r, *sides(pot_x, layer, r))
            adj = slopes(a_x, layer, r, at(a_x, layer - 1, r), at(a_x, layer + 1, r))
            total = sum(p * (a + 0.5 * p) for p, a in zip(pot, adj))
            chosen = mask_x[layer - 1, pl.ds(r, ROWS), :].astype(jnp.float32)
            value = 0.25 * chosen * at(nu_x, layer, r) * total
            term[pl.ds((layer - 1) * cx + r, ROWS), :] = value

    quarter, small = 2 * cx // 4, 2 * cx // 16

    def scatter(mine, index, peer, source, size, box, send, recv):
        return [
            pltpu.make_async_remote_copy(
                src_ref=source.at[pl.ds(pl.multiple_of(index(o) * size, size), size)],
                dst_ref=box.at[o - 1],
                send_sem=send.at[0, o - 1],
                recv_sem=recv.at[0, o - 1],
                device_id=peer(o),
                device_id_type=MESH,
            )
            for o in range(1, 4)
        ]

    def x_peer(o):
        return {"pos": z_lo * 4 + x_index(o)}

    def z_peer(o):
        return {"pos": z_index(o) * 4 + x}

    copies = scatter(x, x_index, x_peer, term, quarter, part_x, x_send, x_recv)
    for copy in copies:
        copy.start()
    for copy in copies:
        copy.wait()

    @pl.loop(0, quarter // ROWS)
    def _(i):
        r = pl.multiple_of(i * ROWS, ROWS)
        own = term[pl.ds(pl.multiple_of(x * quarter + r, ROWS), ROWS), :]
        for o in range(3):
            own += part_x[o, pl.ds(r, ROWS), :]
        piece[pl.ds(r, ROWS), :] = own

    copies = scatter(z_lo, z_index, z_peer, piece, small, part_z, z_send, z_recv)
    for copy in copies:
        copy.start()
    for copy in copies:
        copy.wait()

    own_small = pl.ds(pl.multiple_of(x * quarter + z_lo * small, small), small)
    total = piece[pl.ds(pl.multiple_of(z_lo * small, small), small), :]
    for o in range(3):
        total += part_z[o]
    merged[own_small, :] = total / lax.axis_size("pos")

    def spread(where, peer, send, recv):
        return [
            pltpu.make_async_remote_copy(
                src_ref=merged.at[where],
                dst_ref=merged.at[where],
                send_sem=send.at[1, o - 1],
                recv_sem=recv.at[1, o - 1],
                device_id=peer(o),
                device_id_type=MESH,
            )
            for o in range(1, 4)
        ]

    copies = spread(own_small, z_peer, z_send, z_recv)
    for copy in copies:
        copy.start()
    for copy in copies:
        copy.wait()
    own_quarter = pl.ds(pl.multiple_of(x * quarter, quarter), quarter)
    copies = spread(own_quarter, x_peer, x_send, x_recv)
    for copy in copies:
        copy.start()
    for copy in copies:
        copy.wait()
    outs = [
        pltpu.make_async_copy(merged.at[pl.ds(layer * cx, cx)], gradient.at[layer], out_sem.at[1 + layer])
        for layer in range(2)
    ]
    for copy in outs:
        copy.start()
    for copy in outs:
        copy.wait()
    finish.wait()


def local(labels, magnet_mask, reluctivity, rotor_shift, potential, adjoint_load):
    cx, cy = labels.shape[1:]
    tall = cx + 2 * PAD
    floats = lambda *shape: pltpu.VMEM(shape, jnp.float32)
    sems = pltpu.SemaphoreType.DMA
    return pl.pallas_call(
        kernel,
        out_shape=(
            jax.ShapeDtypeStruct(labels.shape, jnp.float32),
            jax.ShapeDtypeStruct(adjoint_load.shape, jnp.float32),
        ),
        in_specs=[pl.BlockSpec(memory_space=pltpu.SMEM)] * 2 + [pl.BlockSpec(memory_space=pl.ANY)] * 4,
        out_specs=(pl.BlockSpec(memory_space=pl.ANY),) * 2,
        scratch_shapes=[
            pltpu.VMEM((4, cx, cy), jnp.int32),
            floats(4, tall, cy),
            floats(4, tall, cy),
            floats(4, tall, cy),
            floats(4, tall, cy),
            floats(4, tall, cy),
            pltpu.VMEM((2, cx, cy), jnp.int32),
            floats(2 * cx, cy),
            floats(3, cx // 4, cy),
            pltpu.VMEM((cx // 4, cy), jnp.int32),
            floats(2, 8, 128),
            floats(8, 8, 128),
            floats(4, 8, 128),
            floats(3, cx // 2, cy),
            floats(3, cx // 8, cy),
            floats(cx // 2, cy),
            floats(2 * cx, cy),
            sems((4,)),
            sems((4, 3, 4)),
            sems((4, 2, 4)),
            sems((4,)),
            sems((4,)),
            sems((7,)),
            sems((7,)),
            sems((3,)),
            sems((3,)),
            sems((2, 3)),
            sems((2, 3)),
            sems((2, 3)),
            sems((2, 3)),
            sems((3,)),
        ],
        compiler_params=pltpu.CompilerParams(
            collective_id=0, has_side_effects=True, vmem_limit_bytes=60 << 20
        ),
    )(reluctivity, rotor_shift, labels, magnet_mask, potential, adjoint_load)


def solution(mesh):
    return jax.shard_map(
        local,
        mesh=mesh,
        in_specs=(
            P("slab", None, None),
            P("slab", None, None),
            P(),
            P("pos"),
            P("pos", "slab", None, None),
            P("pos", "slab", None, None),
        ),
        out_specs=(P("slab", None, None), P("pos", "slab", None, None)),
        check_vma=False,
    )
```

```python
import jax
import jax.numpy as jnp
from jax import lax
from jax.experimental import pallas as pl
from jax.experimental.pallas import tpu as pltpu
from jax.sharding import PartitionSpec as P

MESH = pl.DeviceIdType.MESH
PAD = 8
ROWS = 32
diagonal_shift = 0.5


def fold(block):
    half = block.shape[1] // 2
    narrow = block[:, :half] + block[:, half:]
    return narrow.reshape(narrow.shape[0] // 8, 8, half).sum(axis=0)


def kernel(
    reluctivity, shift, labels, mask, potential, load, gradient, adjoint,
    label_x, nu_x, d_x, w_x, a_x, pot_x, mask_x, term, relay, relay_label, tile, near, far,
    part_x, part_z, piece, merged, local_sem, send_sem, recv_sem, relay_send, relay_recv,
    near_send, near_recv, far_send, far_recv, x_send, x_recv, z_send, z_recv, out_sem,
):
    pos, slab = lax.axis_index("pos"), lax.axis_index("slab")
    n_slab = lax.axis_size("slab")
    up, down = lax.rem(slab + 1, n_slab), lax.rem(slab + n_slab - 1, n_slab)
    z_hi, inner = slab // 8, lax.rem(slab, 8)
    z_lo, x = pos // 4, lax.rem(pos, 4)
    cx, cy = labels.shape[1], labels.shape[2]

    local = [
        pltpu.make_async_copy(source, target, local_sem.at[i])
        for i, (source, target) in enumerate(
            (
                (load.at[0], d_x.at[pl.ds(1, 2), pl.ds(PAD, cx)]),
                (labels, label_x.at[pl.ds(1, 2)]),
                (potential.at[0], pot_x.at[pl.ds(1, 2), pl.ds(PAD, cx)]),
                (mask, mask_x),
            )
        )
    ]
    for copy in local:
        copy.start()

    def near_peer(o):
        return {"slab": z_hi * 8 + lax.rem(inner + o, 8)}

    def far_peer(o):
        return {"slab": lax.rem(z_hi + o, 4) * 8 + inner}

    def x_index(o):
        return lax.rem(x + o, 4)

    def z_index(o):
        return lax.rem(z_lo + o, 4)

    peers = [{"slab": up}, {"slab": down}]
    peers += [near_peer(o) for o in range(1, 8)]
    peers += [far_peer(o) for o in range(1, 4)]
    peers += [{"pos": z_lo * 4 + x_index(o)} for o in range(1, 4)]
    peers += [{"pos": z_index(o) * 4 + x} for o in range(1, 4)]
    barrier = pltpu.get_barrier_semaphore()

    def greet(peer):
        pl.semaphore_signal(barrier, inc=1, device_id=peer, device_id_type=MESH)

    z_up, z_down = lax.rem(z_hi + 1, 4) * 8, lax.rem(z_hi + 3, 4) * 8
    is_first, is_last = inner == 0, inner == 7
    odd = lax.rem(inner, 2) == 1
    is_up_relay = jnp.logical_and(odd, inner < 7)
    is_down_relay = jnp.logical_and(jnp.logical_not(odd), inner > 0)
    for peer in peers:
        greet(peer)

    @pl.when(is_first)
    def _():
        for i in (1, 3, 5):
            greet({"slab": z_down + i})

    @pl.when(is_last)
    def _():
        for i in (2, 4, 6):
            greet({"slab": z_up + i})

    @pl.when(is_up_relay)
    def _():
        greet({"slab": z_up})

    @pl.when(is_down_relay)
    def _():
        greet({"slab": z_down + 7})

    ends = jnp.logical_or(is_first, is_last)
    pl.semaphore_wait(barrier, len(peers) + jnp.where(ends, 3, 1))
    strip = cx * 7 // 32
    row = inner // 2

    def part(side, k):
        if k == 3 - 3 * side:
            return pl.ds(0 if side else 3 * strip, cx - 3 * strip)
        return pl.ds(k * strip + side * (cx - 4 * strip), strip)

    class Halo:
        def __init__(self, which, first, last, target, buffer):
            def send(source, where, peer, side, k):
                return pltpu.make_async_remote_copy(
                    src_ref=source,
                    dst_ref=where,
                    send_sem=send_sem.at[which, side, k],
                    recv_sem=recv_sem.at[which, side, k],
                    device_id={"slab": peer},
                    device_id_type=MESH,
                )

            def through(source, side, k, peer):
                return pltpu.make_async_remote_copy(
                    src_ref=source.at[part(side, k)],
                    dst_ref=buffer,
                    send_sem=send_sem.at[which, 2, k],
                    recv_sem=relay_recv.at[which],
                    device_id={"slab": peer},
                    device_id_type=MESH,
                )

            def forward(side, ghost, peer):
                first = row * strip + side * (cx - 4 * strip)
                where = pl.ds(pl.multiple_of(first, PAD), strip)
                return pltpu.make_async_remote_copy(
                    src_ref=buffer,
                    dst_ref=target(ghost).at[where],
                    send_sem=relay_send.at[which],
                    recv_sem=recv_sem.at[which, side, row],
                    device_id={"slab": peer},
                    device_id_type=MESH,
                )

            def pieces(source, side, ghost, peer):
                return [
                    send(
                        source.at[part(side, k)],
                        target(ghost).at[part(side, k)],
                        peer, side, k,
                    )
                    for k in range(4)
                ]

            self.whole = [
                (send(last, target(0), up, 0, 0), is_last, is_first),
                (send(first, target(3), down, 1, 0), is_first, is_last),
            ]
            self.parts = [pieces(last, 0, 0, up), pieces(first, 1, 3, down)]
            self.through = [
                [through(last, 0, k, z_hi * 8 + 2 * k + 1) for k in (0, 1, 2)],
                [through(first, 1, k, z_hi * 8 + 2 * k) for k in (1, 2, 3)],
            ]
            self.forward = [
                (is_up_relay, forward(0, 0, z_up)),
                (is_down_relay, forward(1, 3, z_down + 7)),
            ]
            self.arrive = through(last, 0, 0, z_hi * 8)

        def start(self):
            for side, (copy, leaves, _) in enumerate(self.whole):
                direct = self.parts[side][3 - 3 * side]

                @pl.when(leaves)
                def _():
                    for piece in self.through[side]:
                        piece.start()
                    direct.start()

                @pl.when(jnp.logical_not(leaves))
                def _():
                    copy.start()

        def relay(self):
            for role, copy in self.forward:

                @pl.when(role)
                def _():
                    self.arrive.wait_recv()
                    copy.start()

        def wait(self):
            for side, (copy, leaves, enters) in enumerate(self.whole):
                direct = self.parts[side][3 - 3 * side]

                @pl.when(enters)
                def _():
                    for piece in self.parts[side]:
                        piece.wait_recv()

                @pl.when(jnp.logical_not(enters))
                def _():
                    copy.wait_recv()

                @pl.when(leaves)
                def _():
                    for piece in self.through[side]:
                        piece.wait_send()
                    direct.wait_send()

                @pl.when(jnp.logical_not(leaves))
                def _():
                    copy.wait_send()

            for role, copy in self.forward:

                @pl.when(role)
                def _():
                    copy.wait_send()

    def padded(ref):
        return lambda layer: ref.at[layer, pl.ds(PAD, cx)]

    d_halo = Halo(0, load.at[0, 0], load.at[0, 1], padded(d_x), relay.at[0])
    label_halo = Halo(1, labels.at[0], labels.at[1], lambda layer: label_x.at[layer], relay_label)
    pot_halo = Halo(2, potential.at[0, 0], potential.at[0, 1], padded(pot_x), relay.at[1])
    w_halo = Halo(3, padded(w_x)(1), padded(w_x)(2), padded(w_x), relay.at[2])
    label_halo.start()
    d_halo.start()

    for ref in (nu_x, d_x, w_x, a_x, pot_x):
        for layer in (1, 2):
            ref[layer, pl.ds(0, PAD), :] = jnp.zeros((PAD, cy), jnp.float32)
            ref[layer, pl.ds(PAD + cx, PAD), :] = jnp.zeros((PAD, cy), jnp.float32)

    low = jnp.where(slab > 0, 1.0, 0.0)
    high = jnp.where(slab < n_slab - 1, 1.0, 0.0)
    live = (low, 1.0, 1.0, high)
    table = [reluctivity[i] for i in range(4)]
    offset = shift[0]

    def materials(layers):
        def lookup(index):
            result = jnp.where(index == 1, table[1], table[0])
            result = jnp.where(index == 2, table[2], result)
            return jnp.where(index == 3, table[3], result)

        @pl.loop(0, cx // 2 // ROWS)
        def _(i):
            r = pl.multiple_of(i * ROWS, ROWS)
            s = pl.multiple_of(i * ROWS + cx // 2, ROWS)
            for layer in layers:
                turned = pltpu.roll(lookup(label_x[layer, pl.ds(r, ROWS), :]), offset, 1)
                nu_x[layer, pl.ds(PAD + r, ROWS), :] = turned * live[layer]
                still = lookup(label_x[layer, pl.ds(s, ROWS), :])
                nu_x[layer, pl.ds(PAD + s, ROWS), :] = still * live[layer]

    def at(ref, layer, r):
        return ref[layer, pl.ds(PAD + r, ROWS), :]

    def tall(ref, layer, r):
        return ref[layer, pl.ds(r, ROWS + 2 * PAD), :]

    def middle(block):
        return block[PAD : PAD + ROWS]

    def before(block):
        return pltpu.roll(block, 1, 0)

    def after(block):
        return pltpu.roll(block, ROWS + 2 * PAD - 1, 0)

    def operator(ref, layer, r, below, above):
        v_tall, nu_tall = tall(ref, layer, r), tall(nu_x, layer, r)
        flux = 0.5 * (nu_tall + after(nu_tall)) * (v_tall - after(v_tall))
        v, nu = middle(v_tall), middle(nu_tall)
        result = diagonal_shift * v + middle(flux - before(flux))
        for step, other in ((-1, below), (1, above)):
            if other is not None:
                result += 0.5 * (nu + at(nu_x, layer + step, r)) * (v - other)
        flux = 0.5 * (nu + pltpu.roll(nu, cy - 1, 1)) * (v - pltpu.roll(v, cy - 1, 1))
        return v, result + (flux - pltpu.roll(flux, 1, 1))

    zero = jnp.zeros((8, cy // 2), jnp.float32)

    local[1].wait()
    materials((1, 2))
    local[0].wait()

    @pl.loop(0, cx // ROWS)
    def _(i):
        r = pl.multiple_of(i * ROWS, ROWS)
        for layer, others in ((1, (None, at(d_x, 2, r))), (2, (at(d_x, 1, r), None))):
            _, image = operator(d_x, layer, r, *others)
            w_x[layer, pl.ds(PAD + r, ROWS), :] = image

    w_halo.start()
    label_halo.relay()
    d_halo.relay()
    w_halo.relay()
    label_halo.wait()
    materials((0, 3))
    d_halo.wait()
    w_halo.wait()
    pot_halo.start()

    def sides(ref, layer, r):
        below, above = at(ref, layer - 1, r), at(ref, layer + 1, r)
        return (below * low, above) if layer == 1 else (below, above * high)

    def first_pass(i, sums):
        norm, energy = sums
        r = pl.multiple_of(i * ROWS, ROWS)
        for layer, ghost, exists in ((1, 0, low), (2, 3, high)):
            d = at(d_x, layer, r)
            nu = at(nu_x, layer, r) + at(nu_x, ghost, r)
            flux = 0.5 * nu * (d - at(d_x, ghost, r) * exists)
            image = at(w_x, layer, r) + flux
            w_x[layer, pl.ds(PAD + r, ROWS), :] = image
            w_x[ghost, pl.ds(PAD + r, ROWS), :] = at(w_x, ghost, r) - flux
            norm += fold(d * d)
            energy += fold(d * image)
        return norm, energy

    sums = lax.fori_loop(0, cx // ROWS, first_pass, (zero, zero))

    def whole_sum(part):
        return jnp.sum(jnp.sum(part, axis=0, keepdims=True), axis=1, keepdims=True)

    def wide(value, width=cy):
        return jnp.broadcast_to(value[:, :1], (1, width))

    def quotient(top, bottom):
        some = bottom > 0.0
        return jnp.where(some, top / jnp.where(some, bottom, 1.0), 0.0)

    norm, energy = [whole_sum(part) for part in sums]
    theta = quotient(energy, norm)
    theta_wide = wide(theta)
    def second_pass(i, sums):
        m1, m2, m3, m4 = sums
        r = pl.multiple_of(i * ROWS, ROWS)
        for layer in (1, 2):
            w, image = operator(w_x, layer, r, *sides(w_x, layer, r))
            d = at(d_x, layer, r)
            u = w - theta_wide * d
            q = image - theta_wide * w
            m1 += fold(d * u)
            m2 += fold(u * u)
            m3 += fold(u * q)
            m4 += fold(d * q)
        return m1, m2, m3, m4

    sums = lax.fori_loop(0, cx // ROWS, second_pass, (zero,) * 4)

    def combine(box):
        th, m0, m1, m2, m3, m4 = [box[:, i, :] for i in range(6)]
        total = lambda value: jnp.sum(value, axis=0, keepdims=True)
        centre = quotient(total(th * m0 + m1), total(m0))
        e = centre - th
        dw = m1 + th * m0
        return (
            centre,
            total(m0),
            total(m1 - e * m0),
            total(m2 - e * (2.0 * m1 - e * m0)),
            total(m3 - e * (m2 + th * m1 + m4 - e * dw)),
            total(m4 - e * dw),
        )

    def exchange(stage, values, size, mine, box, peer, send, recv):
        for i, value in enumerate(values):
            tile[stage, pl.ds(i, 1), :] = wide(value, tile.shape[2])
        copies = [
            pltpu.make_async_remote_copy(
                src_ref=tile.at[stage],
                dst_ref=box.at[mine],
                send_sem=send.at[o - 1],
                recv_sem=recv.at[o - 1],
                device_id=peer(o),
                device_id_type=MESH,
            )
            for o in range(1, size)
        ]
        for copy in copies:
            copy.start()
        box[mine] = tile[stage]
        for copy in copies:
            copy.wait()
        return combine(box)

    values = (theta, norm, *[whole_sum(part) for part in sums])
    values = exchange(0, values, 8, inner, near, near_peer, near_send, near_recv)
    pot_halo.relay()
    values = exchange(1, values, 4, z_hi, far, far_peer, far_send, far_recv)
    centre, m0, _, m2, m3, _ = values
    alpha0 = 1.0 / centre
    beta = alpha0 * alpha0 * m2 / m0
    alpha1 = m2 / (m3 - alpha0 * m2 * (m2 / m0))
    from_d = wide(alpha0 + alpha1 * (1.0 + beta))
    from_w = wide(alpha0 * alpha1)

    @pl.loop(0, cx // ROWS)
    def _(i):
        r = pl.multiple_of(i * ROWS, ROWS)
        for layer in range(4):
            value = from_d * at(d_x, layer, r) - from_w * at(w_x, layer, r)
            a_x[layer, pl.ds(PAD + r, ROWS), :] = value * live[layer]

    finish = pltpu.make_async_copy(a_x.at[pl.ds(1, 2), pl.ds(PAD, cx)], adjoint.at[0], out_sem.at[0])
    finish.start()
    local[2].wait()
    local[3].wait()
    pot_halo.wait()

    def slopes(ref, layer, r, below, above):
        v_tall = tall(ref, layer, r)
        v = middle(v_tall)
        return (
            above - below,
            middle(after(v_tall) - before(v_tall)),
            pltpu.roll(v, cy - 1, 1) - pltpu.roll(v, 1, 1),
        )

    @pl.loop(0, cx // ROWS)
    def _(i):
        r = pl.multiple_of(i * ROWS, ROWS)
        for layer in (1, 2):
            pot = slopes(pot_x, layer, r, *sides(pot_x, layer, r))
            adj = slopes(a_x, layer, r, at(a_x, layer - 1, r), at(a_x, layer + 1, r))
            total = sum(p * (a + 0.5 * p) for p, a in zip(pot, adj))
            chosen = mask_x[layer - 1, pl.ds(r, ROWS), :].astype(jnp.float32)
            value = 0.25 * chosen * at(nu_x, layer, r) * total
            term[pl.ds((layer - 1) * cx + r, ROWS), :] = value

    quarter, small = 2 * cx // 4, 2 * cx // 16

    def scatter(mine, index, peer, source, size, box, send, recv):
        return [
            pltpu.make_async_remote_copy(
                src_ref=source.at[pl.ds(pl.multiple_of(index(o) * size, size), size)],
                dst_ref=box.at[o - 1],
                send_sem=send.at[0, o - 1],
                recv_sem=recv.at[0, o - 1],
                device_id=peer(o),
                device_id_type=MESH,
            )
            for o in range(1, 4)
        ]

    def x_peer(o):
        return {"pos": z_lo * 4 + x_index(o)}

    def z_peer(o):
        return {"pos": z_index(o) * 4 + x}

    copies = scatter(x, x_index, x_peer, term, quarter, part_x, x_send, x_recv)
    for copy in copies:
        copy.start()
    for copy in copies:
        copy.wait()

    @pl.loop(0, quarter // ROWS)
    def _(i):
        r = pl.multiple_of(i * ROWS, ROWS)
        own = term[pl.ds(pl.multiple_of(x * quarter + r, ROWS), ROWS), :]
        for o in range(3):
            own += part_x[o, pl.ds(r, ROWS), :]
        piece[pl.ds(r, ROWS), :] = own

    copies = scatter(z_lo, z_index, z_peer, piece, small, part_z, z_send, z_recv)
    for copy in copies:
        copy.start()
    for copy in copies:
        copy.wait()

    own_small = pl.ds(pl.multiple_of(x * quarter + z_lo * small, small), small)
    total = piece[pl.ds(pl.multiple_of(z_lo * small, small), small), :]
    for o in range(3):
        total += part_z[o]
    merged[own_small, :] = total / lax.axis_size("pos")

    def spread(where, peer, send, recv):
        return [
            pltpu.make_async_remote_copy(
                src_ref=merged.at[where],
                dst_ref=merged.at[where],
                send_sem=send.at[1, o - 1],
                recv_sem=recv.at[1, o - 1],
                device_id=peer(o),
                device_id_type=MESH,
            )
            for o in range(1, 4)
        ]

    copies = spread(own_small, z_peer, z_send, z_recv)
    for copy in copies:
        copy.start()
    for copy in copies:
        copy.wait()
    own_quarter = pl.ds(pl.multiple_of(x * quarter, quarter), quarter)
    copies = spread(own_quarter, x_peer, x_send, x_recv)
    for copy in copies:
        copy.start()
    for copy in copies:
        copy.wait()
    outs = [
        pltpu.make_async_copy(merged.at[pl.ds(layer * cx, cx)], gradient.at[layer], out_sem.at[1 + layer])
        for layer in range(2)
    ]
    for copy in outs:
        copy.start()
    for copy in outs:
        copy.wait()
    finish.wait()


def local(labels, magnet_mask, reluctivity, rotor_shift, potential, adjoint_load):
    cx, cy = labels.shape[1:]
    tall = cx + 2 * PAD
    floats = lambda *shape: pltpu.VMEM(shape, jnp.float32)
    sems = pltpu.SemaphoreType.DMA
    return pl.pallas_call(
        kernel,
        out_shape=(
            jax.ShapeDtypeStruct(labels.shape, jnp.float32),
            jax.ShapeDtypeStruct(adjoint_load.shape, jnp.float32),
        ),
        in_specs=[pl.BlockSpec(memory_space=pltpu.SMEM)] * 2 + [pl.BlockSpec(memory_space=pl.ANY)] * 4,
        out_specs=(pl.BlockSpec(memory_space=pl.ANY),) * 2,
        scratch_shapes=[
            pltpu.VMEM((4, cx, cy), jnp.int32),
            floats(4, tall, cy),
            floats(4, tall, cy),
            floats(4, tall, cy),
            floats(4, tall, cy),
            floats(4, tall, cy),
            pltpu.VMEM((2, cx, cy), jnp.int32),
            floats(2 * cx, cy),
            floats(3, cx * 7 // 32, cy),
            pltpu.VMEM((cx * 7 // 32, cy), jnp.int32),
            floats(2, 8, 128),
            floats(8, 8, 128),
            floats(4, 8, 128),
            floats(3, cx // 2, cy),
            floats(3, cx // 8, cy),
            floats(cx // 2, cy),
            floats(2 * cx, cy),
            sems((4,)),
            sems((4, 3, 4)),
            sems((4, 2, 4)),
            sems((4,)),
            sems((4,)),
            sems((7,)),
            sems((7,)),
            sems((3,)),
            sems((3,)),
            sems((2, 3)),
            sems((2, 3)),
            sems((2, 3)),
            sems((2, 3)),
            sems((3,)),
        ],
        compiler_params=pltpu.CompilerParams(
            collective_id=0, has_side_effects=True, vmem_limit_bytes=60 << 20
        ),
    )(reluctivity, rotor_shift, labels, magnet_mask, potential, adjoint_load)


def solution(mesh):
    return jax.shard_map(
        local,
        mesh=mesh,
        in_specs=(
            P("slab", None, None),
            P("slab", None, None),
            P(),
            P("pos"),
            P("pos", "slab", None, None),
            P("pos", "slab", None, None),
        ),
        out_specs=(P("slab", None, None), P("pos", "slab", None, None)),
        check_vma=False,
    )
```

```python
import jax
import jax.numpy as jnp
from jax import lax
from jax.experimental import pallas as pl
from jax.experimental.pallas import tpu as pltpu
from jax.sharding import PartitionSpec as P

MESH = pl.DeviceIdType.MESH
PAD = 8
ROWS = 32
diagonal_shift = 0.5


def fold(block):
    half = block.shape[1] // 2
    narrow = block[:, :half] + block[:, half:]
    return narrow.reshape(narrow.shape[0] // 8, 8, half).sum(axis=0)


def kernel(
    reluctivity, shift, labels, mask, potential, load, gradient, adjoint,
    label_x, nu_x, d_x, w_x, a_x, pot_x, mask_x, term, relay, tile, near, far,
    part_x, part_z, piece, merged, local_sem, send_sem, recv_sem, relay_send, relay_recv, share_send, share_recv,
    near_send, near_recv, far_send, far_recv, x_send, x_recv, z_send, z_recv, out_sem,
):
    pos, slab = lax.axis_index("pos"), lax.axis_index("slab")
    n_slab = lax.axis_size("slab")
    up, down = lax.rem(slab + 1, n_slab), lax.rem(slab + n_slab - 1, n_slab)
    z_hi, inner = slab // 8, lax.rem(slab, 8)
    z_lo, x = pos // 4, lax.rem(pos, 4)
    cx, cy = labels.shape[1], labels.shape[2]

    local = [
        pltpu.make_async_copy(source, target, local_sem.at[i])
        for i, (source, target) in enumerate(
            (
                (load.at[0], d_x.at[pl.ds(1, 2), pl.ds(PAD, cx)]),
                (labels, label_x.at[pl.ds(1, 2)]),
                (potential.at[0], pot_x.at[pl.ds(1, 2), pl.ds(PAD, cx)]),
                (mask, mask_x),
            )
        )
    ]
    for copy in local:
        copy.start()

    def near_peer(o):
        return {"slab": z_hi * 8 + lax.rem(inner + o, 8)}

    def far_peer(o):
        return {"slab": lax.rem(z_hi + o, 4) * 8 + inner}

    def x_index(o):
        return lax.rem(x + o, 4)

    def z_index(o):
        return lax.rem(z_lo + o, 4)

    peers = [{"slab": up}, {"slab": down}]
    peers += [near_peer(o) for o in range(1, 8)]
    peers += [far_peer(o) for o in range(1, 4)]
    peers += [{"pos": z_lo * 4 + x_index(o)} for o in range(1, 4)]
    peers += [{"pos": z_index(o) * 4 + x} for o in range(1, 4)]
    barrier = pltpu.get_barrier_semaphore()

    def greet(peer):
        pl.semaphore_signal(barrier, inc=1, device_id=peer, device_id_type=MESH)

    z_up, z_down = lax.rem(z_hi + 1, 4) * 8, lax.rem(z_hi + 3, 4) * 8
    is_first, is_last = inner == 0, inner == 7
    odd = lax.rem(inner, 2) == 1
    is_up_relay = jnp.logical_and(odd, inner < 7)
    is_down_relay = jnp.logical_and(jnp.logical_not(odd), inner > 0)
    for peer in peers:
        greet(peer)

    @pl.when(is_first)
    def _():
        for i in (1, 3, 5):
            greet({"slab": z_down + i})

    @pl.when(is_last)
    def _():
        for i in (2, 4, 6):
            greet({"slab": z_up + i})

    @pl.when(is_up_relay)
    def _():
        greet({"slab": z_up})

    @pl.when(is_down_relay)
    def _():
        greet({"slab": z_down + 7})

    ends = jnp.logical_or(is_first, is_last)
    pl.semaphore_wait(barrier, len(peers) + jnp.where(ends, 3, 1))
    strip = cx // 4
    row = inner // 2

    def part(side, k):
        if k == 3 - 3 * side:
            return pl.ds(0 if side else 3 * strip, cx - 3 * strip)
        return pl.ds(k * strip + side * (cx - 4 * strip), strip)

    class Halo:
        def __init__(self, which, first, last, target, buffer):
            def send(source, where, peer, side, k):
                return pltpu.make_async_remote_copy(
                    src_ref=source,
                    dst_ref=where,
                    send_sem=send_sem.at[which, side, k],
                    recv_sem=recv_sem.at[which, side, k],
                    device_id={"slab": peer},
                    device_id_type=MESH,
                )

            def through(source, side, k, peer):
                return pltpu.make_async_remote_copy(
                    src_ref=source.at[part(side, k)],
                    dst_ref=buffer,
                    send_sem=send_sem.at[which, 2, k],
                    recv_sem=relay_recv.at[which],
                    device_id={"slab": peer},
                    device_id_type=MESH,
                )

            def forward(side, ghost, peer):
                first = row * strip + side * (cx - 4 * strip)
                where = pl.ds(pl.multiple_of(first, PAD), strip)
                return pltpu.make_async_remote_copy(
                    src_ref=buffer,
                    dst_ref=target(ghost).at[where],
                    send_sem=relay_send.at[which],
                    recv_sem=recv_sem.at[which, side, row],
                    device_id={"slab": peer},
                    device_id_type=MESH,
                )

            def pieces(source, side, ghost, peer):
                return [
                    send(
                        source.at[part(side, k)],
                        target(ghost).at[part(side, k)],
                        peer, side, k,
                    )
                    for k in range(4)
                ]

            self.whole = [
                (send(last, target(0), up, 0, 0), is_last, is_first),
                (send(first, target(3), down, 1, 0), is_first, is_last),
            ]
            self.parts = [pieces(last, 0, 0, up), pieces(first, 1, 3, down)]
            self.through = [
                [through(last, 0, k, z_hi * 8 + 2 * k + 1) for k in (0, 1, 2)],
                [through(first, 1, k, z_hi * 8 + 2 * k) for k in (1, 2, 3)],
            ]
            self.forward = [
                (is_up_relay, forward(0, 0, z_up)),
                (is_down_relay, forward(1, 3, z_down + 7)),
            ]
            self.arrive = through(last, 0, 0, z_hi * 8)

        def start(self):
            for side, (copy, leaves, _) in enumerate(self.whole):
                direct = self.parts[side][3 - 3 * side]

                @pl.when(leaves)
                def _():
                    for piece in self.through[side]:
                        piece.start()
                    direct.start()

                @pl.when(jnp.logical_not(leaves))
                def _():
                    copy.start()

        def relay(self):
            for role, copy in self.forward:

                @pl.when(role)
                def _():
                    self.arrive.wait_recv()
                    copy.start()

        def wait(self):
            for side, (copy, leaves, enters) in enumerate(self.whole):
                direct = self.parts[side][3 - 3 * side]

                @pl.when(enters)
                def _():
                    for piece in self.parts[side]:
                        piece.wait_recv()

                @pl.when(jnp.logical_not(enters))
                def _():
                    copy.wait_recv()

                @pl.when(leaves)
                def _():
                    for piece in self.through[side]:
                        piece.wait_send()
                    direct.wait_send()

                @pl.when(jnp.logical_not(leaves))
                def _():
                    copy.wait_send()

            for role, copy in self.forward:

                @pl.when(role)
                def _():
                    copy.wait_send()

    class Shared:
        def __init__(self, which, first, last, target):
            def send(source, where, peer, side):
                return pltpu.make_async_remote_copy(
                    src_ref=source,
                    dst_ref=where,
                    send_sem=send_sem.at[which, side, 0],
                    recv_sem=recv_sem.at[which, side, 0],
                    device_id={"slab": peer},
                    device_id_type=MESH,
                )

            quarter = pl.ds(pl.multiple_of(x * strip, strip), strip)

            def share(ghost, o):
                return pltpu.make_async_remote_copy(
                    src_ref=target(ghost).at[quarter],
                    dst_ref=target(ghost).at[quarter],
                    send_sem=share_send.at[o - 1],
                    recv_sem=share_recv.at[o - 1],
                    device_id={"pos": z_lo * 4 + x_index(o)},
                    device_id_type=MESH,
                )

            self.sides = [
                (
                    send(source, target(ghost), peer, side),
                    send(source.at[quarter], target(ghost).at[quarter], peer, side),
                    [share(ghost, o) for o in range(1, 4)],
                    leaves,
                    enters,
                )
                for side, (source, ghost, peer, leaves, enters) in enumerate(
                    ((last, 0, up, is_last, is_first), (first, 3, down, is_first, is_last))
                )
            ]

        def start(self):
            for whole, quarter, _, leaves, _ in self.sides:

                @pl.when(leaves)
                def _():
                    quarter.start()

                @pl.when(jnp.logical_not(leaves))
                def _():
                    whole.start()

        def relay(self):
            for _, quarter, shares, _, enters in self.sides:

                @pl.when(enters)
                def _():
                    quarter.wait_recv()
                    for share in shares:
                        share.start()

        def wait(self):
            for whole, quarter, shares, leaves, enters in self.sides:

                @pl.when(enters)
                def _():
                    for share in shares:
                        share.wait()

                @pl.when(jnp.logical_not(enters))
                def _():
                    whole.wait_recv()

                @pl.when(leaves)
                def _():
                    quarter.wait_send()

                @pl.when(jnp.logical_not(leaves))
                def _():
                    whole.wait_send()

    def padded(ref):
        return lambda layer: ref.at[layer, pl.ds(PAD, cx)]

    d_halo = Halo(0, load.at[0, 0], load.at[0, 1], padded(d_x), relay.at[0])
    label_halo = Shared(1, labels.at[0], labels.at[1], lambda layer: label_x.at[layer])
    pot_halo = Halo(2, potential.at[0, 0], potential.at[0, 1], padded(pot_x), relay.at[1])
    w_halo = Halo(3, padded(w_x)(1), padded(w_x)(2), padded(w_x), relay.at[2])
    label_halo.start()
    d_halo.start()

    for ref in (nu_x, d_x, w_x, a_x, pot_x):
        for layer in (1, 2):
            ref[layer, pl.ds(0, PAD), :] = jnp.zeros((PAD, cy), jnp.float32)
            ref[layer, pl.ds(PAD + cx, PAD), :] = jnp.zeros((PAD, cy), jnp.float32)

    low = jnp.where(slab > 0, 1.0, 0.0)
    high = jnp.where(slab < n_slab - 1, 1.0, 0.0)
    live = (low, 1.0, 1.0, high)
    table = [reluctivity[i] for i in range(4)]
    offset = shift[0]

    def materials(layers):
        def lookup(index):
            result = jnp.where(index == 1, table[1], table[0])
            result = jnp.where(index == 2, table[2], result)
            return jnp.where(index == 3, table[3], result)

        @pl.loop(0, cx // 2 // ROWS)
        def _(i):
            r = pl.multiple_of(i * ROWS, ROWS)
            s = pl.multiple_of(i * ROWS + cx // 2, ROWS)
            for layer in layers:
                turned = pltpu.roll(lookup(label_x[layer, pl.ds(r, ROWS), :]), offset, 1)
                nu_x[layer, pl.ds(PAD + r, ROWS), :] = turned * live[layer]
                still = lookup(label_x[layer, pl.ds(s, ROWS), :])
                nu_x[layer, pl.ds(PAD + s, ROWS), :] = still * live[layer]

    def at(ref, layer, r):
        return ref[layer, pl.ds(PAD + r, ROWS), :]

    def tall(ref, layer, r):
        return ref[layer, pl.ds(r, ROWS + 2 * PAD), :]

    def middle(block):
        return block[PAD : PAD + ROWS]

    def before(block):
        return pltpu.roll(block, 1, 0)

    def after(block):
        return pltpu.roll(block, ROWS + 2 * PAD - 1, 0)

    def operator(ref, layer, r, below, above):
        v_tall, nu_tall = tall(ref, layer, r), tall(nu_x, layer, r)
        flux = 0.5 * (nu_tall + after(nu_tall)) * (v_tall - after(v_tall))
        v, nu = middle(v_tall), middle(nu_tall)
        result = diagonal_shift * v + middle(flux - before(flux))
        for step, other in ((-1, below), (1, above)):
            if other is not None:
                result += 0.5 * (nu + at(nu_x, layer + step, r)) * (v - other)
        flux = 0.5 * (nu + pltpu.roll(nu, cy - 1, 1)) * (v - pltpu.roll(v, cy - 1, 1))
        return v, result + (flux - pltpu.roll(flux, 1, 1))

    zero = jnp.zeros((8, cy // 2), jnp.float32)

    local[1].wait()
    materials((1, 2))
    local[0].wait()

    @pl.loop(0, cx // ROWS)
    def _(i):
        r = pl.multiple_of(i * ROWS, ROWS)
        for layer, others in ((1, (None, at(d_x, 2, r))), (2, (at(d_x, 1, r), None))):
            _, image = operator(d_x, layer, r, *others)
            w_x[layer, pl.ds(PAD + r, ROWS), :] = image

    w_halo.start()
    label_halo.relay()
    d_halo.relay()
    w_halo.relay()
    label_halo.wait()
    materials((0, 3))
    d_halo.wait()
    w_halo.wait()
    pot_halo.start()

    def sides(ref, layer, r):
        below, above = at(ref, layer - 1, r), at(ref, layer + 1, r)
        return (below * low, above) if layer == 1 else (below, above * high)

    def first_pass(i, sums):
        norm, energy = sums
        r = pl.multiple_of(i * ROWS, ROWS)
        for layer, ghost, exists in ((1, 0, low), (2, 3, high)):
            d = at(d_x, layer, r)
            nu = at(nu_x, layer, r) + at(nu_x, ghost, r)
            flux = 0.5 * nu * (d - at(d_x, ghost, r) * exists)
            image = at(w_x, layer, r) + flux
            w_x[layer, pl.ds(PAD + r, ROWS), :] = image
            w_x[ghost, pl.ds(PAD + r, ROWS), :] = at(w_x, ghost, r) - flux
            norm += fold(d * d)
            energy += fold(d * image)
        return norm, energy

    sums = lax.fori_loop(0, cx // ROWS, first_pass, (zero, zero))

    def whole_sum(part):
        return jnp.sum(jnp.sum(part, axis=0, keepdims=True), axis=1, keepdims=True)

    def wide(value, width=cy):
        return jnp.broadcast_to(value[:, :1], (1, width))

    def quotient(top, bottom):
        some = bottom > 0.0
        return jnp.where(some, top / jnp.where(some, bottom, 1.0), 0.0)

    norm, energy = [whole_sum(part) for part in sums]
    theta = quotient(energy, norm)
    theta_wide = wide(theta)
    def second_pass(i, sums):
        m1, m2, m3, m4 = sums
        r = pl.multiple_of(i * ROWS, ROWS)
        for layer in (1, 2):
            w, image = operator(w_x, layer, r, *sides(w_x, layer, r))
            d = at(d_x, layer, r)
            u = w - theta_wide * d
            q = image - theta_wide * w
            m1 += fold(d * u)
            m2 += fold(u * u)
            m3 += fold(u * q)
            m4 += fold(d * q)
        return m1, m2, m3, m4

    sums = lax.fori_loop(0, cx // ROWS, second_pass, (zero,) * 4)

    def combine(box):
        th, m0, m1, m2, m3, m4 = [box[:, i, :] for i in range(6)]
        total = lambda value: jnp.sum(value, axis=0, keepdims=True)
        centre = quotient(total(th * m0 + m1), total(m0))
        e = centre - th
        dw = m1 + th * m0
        return (
            centre,
            total(m0),
            total(m1 - e * m0),
            total(m2 - e * (2.0 * m1 - e * m0)),
            total(m3 - e * (m2 + th * m1 + m4 - e * dw)),
            total(m4 - e * dw),
        )

    def exchange(stage, values, size, mine, box, peer, send, recv):
        for i, value in enumerate(values):
            tile[stage, pl.ds(i, 1), :] = wide(value, tile.shape[2])
        copies = [
            pltpu.make_async_remote_copy(
                src_ref=tile.at[stage],
                dst_ref=box.at[mine],
                send_sem=send.at[o - 1],
                recv_sem=recv.at[o - 1],
                device_id=peer(o),
                device_id_type=MESH,
            )
            for o in range(1, size)
        ]
        for copy in copies:
            copy.start()
        box[mine] = tile[stage]
        for copy in copies:
            copy.wait()
        return combine(box)

    values = (theta, norm, *[whole_sum(part) for part in sums])
    values = exchange(0, values, 8, inner, near, near_peer, near_send, near_recv)
    pot_halo.relay()
    values = exchange(1, values, 4, z_hi, far, far_peer, far_send, far_recv)
    centre, m0, _, m2, m3, _ = values
    alpha0 = 1.0 / centre
    beta = alpha0 * alpha0 * m2 / m0
    alpha1 = m2 / (m3 - alpha0 * m2 * (m2 / m0))
    from_d = wide(alpha0 + alpha1 * (1.0 + beta))
    from_w = wide(alpha0 * alpha1)

    @pl.loop(0, cx // ROWS)
    def _(i):
        r = pl.multiple_of(i * ROWS, ROWS)
        for layer in range(4):
            value = from_d * at(d_x, layer, r) - from_w * at(w_x, layer, r)
            a_x[layer, pl.ds(PAD + r, ROWS), :] = value * live[layer]

    finish = pltpu.make_async_copy(a_x.at[pl.ds(1, 2), pl.ds(PAD, cx)], adjoint.at[0], out_sem.at[0])
    finish.start()
    local[2].wait()
    local[3].wait()
    pot_halo.wait()

    def slopes(ref, layer, r, below, above):
        v_tall = tall(ref, layer, r)
        v = middle(v_tall)
        return (
            above - below,
            middle(after(v_tall) - before(v_tall)),
            pltpu.roll(v, cy - 1, 1) - pltpu.roll(v, 1, 1),
        )

    @pl.loop(0, cx // ROWS)
    def _(i):
        r = pl.multiple_of(i * ROWS, ROWS)
        for layer in (1, 2):
            pot = slopes(pot_x, layer, r, *sides(pot_x, layer, r))
            adj = slopes(a_x, layer, r, at(a_x, layer - 1, r), at(a_x, layer + 1, r))
            total = sum(p * (a + 0.5 * p) for p, a in zip(pot, adj))
            chosen = mask_x[layer - 1, pl.ds(r, ROWS), :].astype(jnp.float32)
            value = 0.25 * chosen * at(nu_x, layer, r) * total
            term[pl.ds((layer - 1) * cx + r, ROWS), :] = value

    quarter, small = 2 * cx // 4, 2 * cx // 16

    def scatter(mine, index, peer, source, size, box, send, recv):
        return [
            pltpu.make_async_remote_copy(
                src_ref=source.at[pl.ds(pl.multiple_of(index(o) * size, size), size)],
                dst_ref=box.at[o - 1],
                send_sem=send.at[0, o - 1],
                recv_sem=recv.at[0, o - 1],
                device_id=peer(o),
                device_id_type=MESH,
            )
            for o in range(1, 4)
        ]

    def x_peer(o):
        return {"pos": z_lo * 4 + x_index(o)}

    def z_peer(o):
        return {"pos": z_index(o) * 4 + x}

    copies = scatter(x, x_index, x_peer, term, quarter, part_x, x_send, x_recv)
    for copy in copies:
        copy.start()
    for copy in copies:
        copy.wait()

    @pl.loop(0, quarter // ROWS)
    def _(i):
        r = pl.multiple_of(i * ROWS, ROWS)
        own = term[pl.ds(pl.multiple_of(x * quarter + r, ROWS), ROWS), :]
        for o in range(3):
            own += part_x[o, pl.ds(r, ROWS), :]
        piece[pl.ds(r, ROWS), :] = own

    copies = scatter(z_lo, z_index, z_peer, piece, small, part_z, z_send, z_recv)
    for copy in copies:
        copy.start()
    for copy in copies:
        copy.wait()

    own_small = pl.ds(pl.multiple_of(z_lo * small, small), small)
    total = piece[own_small, :]
    for o in range(3):
        total += part_z[o]
    merged[own_small, :] = total / lax.axis_size("pos")
    own_quarter = gradient.at[x // 2, pl.ds(pl.multiple_of(lax.rem(x, 2) * quarter, quarter), quarter)]

    def spread(source, target, peer, send, recv):
        copies = [
            pltpu.make_async_remote_copy(
                src_ref=source,
                dst_ref=target,
                send_sem=send.at[1, o - 1],
                recv_sem=recv.at[1, o - 1],
                device_id=peer(o),
                device_id_type=MESH,
            )
            for o in range(1, 4)
        ]
        for copy in copies:
            copy.start()
        return copies

    for copy in spread(merged.at[own_small], merged.at[own_small], z_peer, z_send, z_recv):
        copy.wait()
    copies = spread(merged, own_quarter, x_peer, x_send, x_recv)
    keep = pltpu.make_async_copy(merged, own_quarter, out_sem.at[1])
    keep.start()
    for copy in copies:
        copy.wait()
    keep.wait()
    finish.wait()


def local(labels, magnet_mask, reluctivity, rotor_shift, potential, adjoint_load):
    cx, cy = labels.shape[1:]
    tall = cx + 2 * PAD
    floats = lambda *shape: pltpu.VMEM(shape, jnp.float32)
    sems = pltpu.SemaphoreType.DMA
    return pl.pallas_call(
        kernel,
        out_shape=(
            jax.ShapeDtypeStruct(labels.shape, jnp.float32),
            jax.ShapeDtypeStruct(adjoint_load.shape, jnp.float32),
        ),
        in_specs=[pl.BlockSpec(memory_space=pltpu.SMEM)] * 2 + [pl.BlockSpec(memory_space=pltpu.HBM)] * 4,
        out_specs=(pl.BlockSpec(memory_space=pl.ANY),) * 2,
        scratch_shapes=[
            pltpu.VMEM((4, cx, cy), jnp.int32),
            floats(4, tall, cy),
            floats(4, tall, cy),
            floats(4, tall, cy),
            floats(4, tall, cy),
            floats(4, tall, cy),
            pltpu.VMEM((2, cx, cy), jnp.int32),
            floats(2 * cx, cy),
            floats(3, cx // 4, cy),
            floats(2, 8, 128),
            floats(8, 8, 128),
            floats(4, 8, 128),
            floats(3, cx // 2, cy),
            floats(3, cx // 8, cy),
            floats(cx // 2, cy),
            floats(cx // 2, cy),
            sems((4,)),
            sems((4, 3, 4)),
            sems((4, 2, 4)),
            sems((4,)),
            sems((4,)),
            sems((3,)),
            sems((3,)),
            sems((7,)),
            sems((7,)),
            sems((3,)),
            sems((3,)),
            sems((2, 3)),
            sems((2, 3)),
            sems((2, 3)),
            sems((2, 3)),
            sems((2,)),
        ],
        compiler_params=pltpu.CompilerParams(
            collective_id=0, has_side_effects=True, vmem_limit_bytes=24 << 20
        ),
    )(reluctivity, rotor_shift, *[pltpu.with_memory_space_constraint(v, pltpu.HBM) for v in (labels, magnet_mask, potential, adjoint_load)])


def solution(mesh):
    return jax.shard_map(
        local,
        mesh=mesh,
        in_specs=(
            P("slab", None, None),
            P("slab", None, None),
            P(),
            P("pos"),
            P("pos", "slab", None, None),
            P("pos", "slab", None, None),
        ),
        out_specs=(P("slab", None, None), P("pos", "slab", None, None)),
        check_vma=False,
    )
```

```python
import jax
import jax.numpy as jnp
from jax import lax
from jax.experimental import pallas as pl
from jax.experimental.pallas import tpu as pltpu
from jax.sharding import PartitionSpec as P

MESH = pl.DeviceIdType.MESH
PAD = 8
ROWS = 32
diagonal_shift = 0.5


def fold(block):
    half = block.shape[1] // 2
    narrow = block[:, :half] + block[:, half:]
    return narrow.reshape(narrow.shape[0] // 8, 8, half).sum(axis=0)


def kernel(
    reluctivity, shift, labels, mask, potential, load, gradient, adjoint,
    label_x, nu_x, d_x, w_x, a_x, pot_x, mask_x, term, relay, tile, near, far,
    part_x, part_z, piece, merged, local_sem, send_sem, recv_sem, relay_send, relay_recv, share_send, share_recv,
    near_send, near_recv, far_send, far_recv, x_send, x_recv, z_send, z_recv, out_sem,
):
    pos, slab = lax.axis_index("pos"), lax.axis_index("slab")
    n_slab = lax.axis_size("slab")
    up, down = lax.rem(slab + 1, n_slab), lax.rem(slab + n_slab - 1, n_slab)
    z_hi, inner = slab // 8, lax.rem(slab, 8)
    z_lo, x = pos // 4, lax.rem(pos, 4)
    cx, cy = labels.shape[1], labels.shape[2]

    local = [
        pltpu.make_async_copy(source, target, local_sem.at[i])
        for i, (source, target) in enumerate(
            (
                (load.at[0], d_x.at[pl.ds(1, 2), pl.ds(PAD, cx)]),
                (labels, label_x.at[pl.ds(1, 2)]),
                (potential.at[0], pot_x.at[pl.ds(1, 2), pl.ds(PAD, cx)]),
                (mask, mask_x),
            )
        )
    ]
    for copy in local:
        copy.start()

    def near_peer(o):
        return {"slab": z_hi * 8 + lax.rem(inner + o, 8)}

    def far_peer(o):
        return {"slab": lax.rem(z_hi + o, 4) * 8 + inner}

    def x_index(o):
        return lax.rem(x + o, 4)

    def z_index(o):
        return lax.rem(z_lo + o, 4)

    peers = [{"slab": up}, {"slab": down}]
    peers += [near_peer(o) for o in range(1, 8)]
    peers += [far_peer(o) for o in range(1, 4)]
    peers += [{"pos": z_lo * 4 + x_index(o)} for o in range(1, 4)]
    peers += [{"pos": z_index(o) * 4 + x} for o in range(1, 4)]
    barrier = pltpu.get_barrier_semaphore()

    def greet(peer):
        pl.semaphore_signal(barrier, inc=1, device_id=peer, device_id_type=MESH)

    z_up, z_down = lax.rem(z_hi + 1, 4) * 8, lax.rem(z_hi + 3, 4) * 8
    is_first, is_last = inner == 0, inner == 7
    odd = lax.rem(inner, 2) == 1
    is_up_relay = jnp.logical_and(odd, inner < 7)
    is_down_relay = jnp.logical_and(jnp.logical_not(odd), inner > 0)
    for peer in peers:
        greet(peer)

    @pl.when(is_first)
    def _():
        for i in (1, 3, 5):
            greet({"slab": z_down + i})

    @pl.when(is_last)
    def _():
        for i in (2, 4, 6):
            greet({"slab": z_up + i})

    @pl.when(is_up_relay)
    def _():
        greet({"slab": z_up})

    @pl.when(is_down_relay)
    def _():
        greet({"slab": z_down + 7})

    ends = jnp.logical_or(is_first, is_last)
    pl.semaphore_wait(barrier, len(peers) + jnp.where(ends, 3, 1))
    strip = cx // 4
    row = inner // 2

    def part(side, k):
        if k == 3 - 3 * side:
            return pl.ds(0 if side else 3 * strip, cx - 3 * strip)
        return pl.ds(k * strip + side * (cx - 4 * strip), strip)

    class Halo:
        def __init__(self, which, first, last, target, buffer):
            def send(source, where, peer, side, k):
                return pltpu.make_async_remote_copy(
                    src_ref=source,
                    dst_ref=where,
                    send_sem=send_sem.at[which, side, k],
                    recv_sem=recv_sem.at[which, side, k],
                    device_id={"slab": peer},
                    device_id_type=MESH,
                )

            def through(source, side, k, peer):
                return pltpu.make_async_remote_copy(
                    src_ref=source.at[part(side, k)],
                    dst_ref=buffer,
                    send_sem=send_sem.at[which, 2, k],
                    recv_sem=relay_recv.at[which],
                    device_id={"slab": peer},
                    device_id_type=MESH,
                )

            def forward(side, ghost, peer):
                first = row * strip + side * (cx - 4 * strip)
                where = pl.ds(pl.multiple_of(first, PAD), strip)
                return pltpu.make_async_remote_copy(
                    src_ref=buffer,
                    dst_ref=target(ghost).at[where],
                    send_sem=relay_send.at[which],
                    recv_sem=recv_sem.at[which, side, row],
                    device_id={"slab": peer},
                    device_id_type=MESH,
                )

            def pieces(source, side, ghost, peer):
                return [
                    send(
                        source.at[part(side, k)],
                        target(ghost).at[part(side, k)],
                        peer, side, k,
                    )
                    for k in range(4)
                ]

            self.whole = [
                (send(last, target(0), up, 0, 0), is_last, is_first),
                (send(first, target(3), down, 1, 0), is_first, is_last),
            ]
            self.parts = [pieces(last, 0, 0, up), pieces(first, 1, 3, down)]
            self.through = [
                [through(last, 0, k, z_hi * 8 + 2 * k + 1) for k in (0, 1, 2)],
                [through(first, 1, k, z_hi * 8 + 2 * k) for k in (1, 2, 3)],
            ]
            self.forward = [
                (is_up_relay, forward(0, 0, z_up)),
                (is_down_relay, forward(1, 3, z_down + 7)),
            ]
            self.arrive = through(last, 0, 0, z_hi * 8)

        def start(self):
            for side, (copy, leaves, _) in enumerate(self.whole):
                direct = self.parts[side][3 - 3 * side]

                @pl.when(leaves)
                def _():
                    for piece in self.through[side]:
                        piece.start()
                    direct.start()

                @pl.when(jnp.logical_not(leaves))
                def _():
                    copy.start()

        def relay(self):
            for role, copy in self.forward:

                @pl.when(role)
                def _():
                    self.arrive.wait_recv()
                    copy.start()

        def wait(self):
            for side, (copy, leaves, enters) in enumerate(self.whole):
                direct = self.parts[side][3 - 3 * side]

                @pl.when(enters)
                def _():
                    for piece in self.parts[side]:
                        piece.wait_recv()

                @pl.when(jnp.logical_not(enters))
                def _():
                    copy.wait_recv()

                @pl.when(leaves)
                def _():
                    for piece in self.through[side]:
                        piece.wait_send()
                    direct.wait_send()

                @pl.when(jnp.logical_not(leaves))
                def _():
                    copy.wait_send()

            for role, copy in self.forward:

                @pl.when(role)
                def _():
                    copy.wait_send()

    class Shared:
        def __init__(self, which, first, last, target):
            def send(source, where, peer, side):
                return pltpu.make_async_remote_copy(
                    src_ref=source,
                    dst_ref=where,
                    send_sem=send_sem.at[which, side, 0],
                    recv_sem=recv_sem.at[which, side, 0],
                    device_id={"slab": peer},
                    device_id_type=MESH,
                )

            quarter = pl.ds(pl.multiple_of(x * strip, strip), strip)

            def share(ghost, o):
                return pltpu.make_async_remote_copy(
                    src_ref=target(ghost).at[quarter],
                    dst_ref=target(ghost).at[quarter],
                    send_sem=share_send.at[o - 1],
                    recv_sem=share_recv.at[o - 1],
                    device_id={"pos": z_lo * 4 + x_index(o)},
                    device_id_type=MESH,
                )

            self.sides = [
                (
                    send(source, target(ghost), peer, side),
                    send(source.at[quarter], target(ghost).at[quarter], peer, side),
                    [share(ghost, o) for o in range(1, 4)],
                    leaves,
                    enters,
                )
                for side, (source, ghost, peer, leaves, enters) in enumerate(
                    ((last, 0, up, is_last, is_first), (first, 3, down, is_first, is_last))
                )
            ]

        def start(self):
            for whole, quarter, _, leaves, _ in self.sides:

                @pl.when(leaves)
                def _():
                    quarter.start()

                @pl.when(jnp.logical_not(leaves))
                def _():
                    whole.start()

        def relay(self):
            for _, quarter, shares, _, enters in self.sides:

                @pl.when(enters)
                def _():
                    quarter.wait_recv()
                    for share in shares:
                        share.start()

        def wait(self):
            for whole, quarter, shares, leaves, enters in self.sides:

                @pl.when(enters)
                def _():
                    for share in shares:
                        share.wait()

                @pl.when(jnp.logical_not(enters))
                def _():
                    whole.wait_recv()

                @pl.when(leaves)
                def _():
                    quarter.wait_send()

                @pl.when(jnp.logical_not(leaves))
                def _():
                    whole.wait_send()

    def padded(ref):
        return lambda layer: ref.at[layer, pl.ds(PAD, cx)]

    d_halo = Halo(0, load.at[0, 0], load.at[0, 1], padded(d_x), relay.at[0])
    label_halo = Shared(1, labels.at[0], labels.at[1], lambda layer: label_x.at[layer])
    pot_halo = Halo(2, potential.at[0, 0], potential.at[0, 1], padded(pot_x), relay.at[1])
    w_halo = Halo(3, padded(w_x)(1), padded(w_x)(2), padded(w_x), relay.at[2])
    label_halo.start()
    d_halo.start()

    for ref in (nu_x, d_x, w_x, a_x, pot_x):
        for layer in (1, 2):
            ref[layer, pl.ds(0, PAD), :] = jnp.zeros((PAD, cy), jnp.float32)
            ref[layer, pl.ds(PAD + cx, PAD), :] = jnp.zeros((PAD, cy), jnp.float32)

    low = jnp.where(slab > 0, 1.0, 0.0)
    high = jnp.where(slab < n_slab - 1, 1.0, 0.0)
    live = (low, 1.0, 1.0, high)
    table = [reluctivity[i] for i in range(4)]
    offset = shift[0]

    def materials(layers):
        def lookup(index):
            result = jnp.where(index == 1, table[1], table[0])
            result = jnp.where(index == 2, table[2], result)
            return jnp.where(index == 3, table[3], result)

        @pl.loop(0, cx // 2 // ROWS)
        def _(i):
            r = pl.multiple_of(i * ROWS, ROWS)
            s = pl.multiple_of(i * ROWS + cx // 2, ROWS)
            for layer in layers:
                turned = pltpu.roll(lookup(label_x[layer, pl.ds(r, ROWS), :]), offset, 1)
                nu_x[layer, pl.ds(PAD + r, ROWS), :] = turned * live[layer]
                still = lookup(label_x[layer, pl.ds(s, ROWS), :])
                nu_x[layer, pl.ds(PAD + s, ROWS), :] = still * live[layer]

    def at(ref, layer, r):
        return ref[layer, pl.ds(PAD + r, ROWS), :]

    def tall(ref, layer, r):
        return ref[layer, pl.ds(r, ROWS + 2 * PAD), :]

    def middle(block):
        return block[PAD : PAD + ROWS]

    def before(block):
        return pltpu.roll(block, 1, 0)

    def after(block):
        return pltpu.roll(block, ROWS + 2 * PAD - 1, 0)

    def operator(ref, layer, r, below, above):
        v_tall, nu_tall = tall(ref, layer, r), tall(nu_x, layer, r)
        flux = 0.5 * (nu_tall + after(nu_tall)) * (v_tall - after(v_tall))
        v, nu = middle(v_tall), middle(nu_tall)
        result = diagonal_shift * v + middle(flux - before(flux))
        for step, other in ((-1, below), (1, above)):
            if other is not None:
                result += 0.5 * (nu + at(nu_x, layer + step, r)) * (v - other)
        flux = 0.5 * (nu + pltpu.roll(nu, cy - 1, 1)) * (v - pltpu.roll(v, cy - 1, 1))
        return v, result + (flux - pltpu.roll(flux, 1, 1))

    zero = jnp.zeros((8, cy // 2), jnp.float32)

    local[1].wait()
    materials((1, 2))
    local[0].wait()

    @pl.loop(0, cx // ROWS)
    def _(i):
        r = pl.multiple_of(i * ROWS, ROWS)
        for layer, others in ((1, (None, at(d_x, 2, r))), (2, (at(d_x, 1, r), None))):
            _, image = operator(d_x, layer, r, *others)
            w_x[layer, pl.ds(PAD + r, ROWS), :] = image

    w_halo.start()
    label_halo.relay()
    d_halo.relay()
    w_halo.relay()
    label_halo.wait()
    materials((0, 3))
    d_halo.wait()
    w_halo.wait()
    pot_halo.start()

    def sides(ref, layer, r):
        below, above = at(ref, layer - 1, r), at(ref, layer + 1, r)
        return (below * low, above) if layer == 1 else (below, above * high)

    def first_pass(i, sums):
        norm, energy = sums
        r = pl.multiple_of(i * ROWS, ROWS)
        for layer, ghost, exists in ((1, 0, low), (2, 3, high)):
            d = at(d_x, layer, r)
            nu = at(nu_x, layer, r) + at(nu_x, ghost, r)
            flux = 0.5 * nu * (d - at(d_x, ghost, r) * exists)
            image = at(w_x, layer, r) + flux
            w_x[layer, pl.ds(PAD + r, ROWS), :] = image
            w_x[ghost, pl.ds(PAD + r, ROWS), :] = at(w_x, ghost, r) - flux
            norm += fold(d * d)
            energy += fold(d * image)
        return norm, energy

    sums = lax.fori_loop(0, cx // ROWS, first_pass, (zero, zero))

    def whole_sum(part):
        return jnp.sum(jnp.sum(part, axis=0, keepdims=True), axis=1, keepdims=True)

    def wide(value, width=cy):
        return jnp.broadcast_to(value[:, :1], (1, width))

    def quotient(top, bottom):
        some = bottom > 0.0
        return jnp.where(some, top / jnp.where(some, bottom, 1.0), 0.0)

    norm, energy = [whole_sum(part) for part in sums]
    theta = quotient(energy, norm)
    theta_wide = wide(theta)
    def second_pass(i, sums):
        m1, m2, m3, m4 = sums
        r = pl.multiple_of(i * ROWS, ROWS)
        for layer in (1, 2):
            w, image = operator(w_x, layer, r, *sides(w_x, layer, r))
            d = at(d_x, layer, r)
            u = w - theta_wide * d
            q = image - theta_wide * w
            m1 += fold(d * u)
            m2 += fold(u * u)
            m3 += fold(u * q)
            m4 += fold(d * q)
        return m1, m2, m3, m4

    sums = lax.fori_loop(0, cx // ROWS, second_pass, (zero,) * 4)

    def combine(box):
        th, m0, m1, m2, m3, m4 = [box[:, i, :] for i in range(6)]
        total = lambda value: jnp.sum(value, axis=0, keepdims=True)
        centre = quotient(total(th * m0 + m1), total(m0))
        e = centre - th
        dw = m1 + th * m0
        return (
            centre,
            total(m0),
            total(m1 - e * m0),
            total(m2 - e * (2.0 * m1 - e * m0)),
            total(m3 - e * (m2 + th * m1 + m4 - e * dw)),
            total(m4 - e * dw),
        )

    def exchange(stage, values, size, mine, box, peer, send, recv):
        for i, value in enumerate(values):
            tile[stage, pl.ds(i, 1), :] = wide(value, tile.shape[2])
        copies = [
            pltpu.make_async_remote_copy(
                src_ref=tile.at[stage],
                dst_ref=box.at[mine],
                send_sem=send.at[o - 1],
                recv_sem=recv.at[o - 1],
                device_id=peer(o),
                device_id_type=MESH,
            )
            for o in range(1, size)
        ]
        for copy in copies:
            copy.start()
        box[mine] = tile[stage]
        for copy in copies:
            copy.wait()
        return combine(box)

    values = (theta, norm, *[whole_sum(part) for part in sums])
    values = exchange(0, values, 8, inner, near, near_peer, near_send, near_recv)
    pot_halo.relay()
    values = exchange(1, values, 4, z_hi, far, far_peer, far_send, far_recv)
    centre, m0, _, m2, m3, _ = values
    alpha0 = 1.0 / centre
    beta = alpha0 * alpha0 * m2 / m0
    alpha1 = m2 / (m3 - alpha0 * m2 * (m2 / m0))
    from_d = wide(alpha0 + alpha1 * (1.0 + beta))
    from_w = wide(alpha0 * alpha1)

    @pl.loop(0, cx // ROWS)
    def _(i):
        r = pl.multiple_of(i * ROWS, ROWS)
        for layer in range(4):
            value = from_d * at(d_x, layer, r) - from_w * at(w_x, layer, r)
            a_x[layer, pl.ds(PAD + r, ROWS), :] = value * live[layer]

    finish = pltpu.make_async_copy(a_x.at[pl.ds(1, 2), pl.ds(PAD, cx)], adjoint.at[0], out_sem.at[0])
    finish.start()
    local[2].wait()
    local[3].wait()
    pot_halo.wait()

    def slopes(ref, layer, r, below, above):
        v_tall = tall(ref, layer, r)
        v = middle(v_tall)
        return (
            above - below,
            middle(after(v_tall) - before(v_tall)),
            pltpu.roll(v, cy - 1, 1) - pltpu.roll(v, 1, 1),
        )

    @pl.loop(0, cx // ROWS)
    def _(i):
        r = pl.multiple_of(i * ROWS, ROWS)
        for layer in (1, 2):
            pot = slopes(pot_x, layer, r, *sides(pot_x, layer, r))
            adj = slopes(a_x, layer, r, at(a_x, layer - 1, r), at(a_x, layer + 1, r))
            total = sum(p * (a + 0.5 * p) for p, a in zip(pot, adj))
            chosen = mask_x[layer - 1, pl.ds(r, ROWS), :].astype(jnp.float32)
            value = 0.25 * chosen * at(nu_x, layer, r) * total
            term[pl.ds((layer - 1) * cx + r, ROWS), :] = value

    quarter, small = 2 * cx // 4, 2 * cx // 16

    def x_peer(o):
        return {"pos": z_lo * 4 + x_index(o)}

    def z_peer(o):
        return {"pos": z_index(o) * 4 + x}

    def remote(source, target, send, recv, peer):
        return pltpu.make_async_remote_copy(
            src_ref=source, dst_ref=target, send_sem=send, recv_sem=recv, device_id=peer, device_id_type=MESH
        )

    def rows_of(index):
        return pl.ds(pl.multiple_of(index * small, small), small)

    order = (1, 2, 3, 0)
    along_x = {
        oz: [
            remote(
                term.at[rows_of(x_index(o) * 4 + z_index(oz))],
                part_x.at[o - 1, rows_of(z_index(oz))],
                x_send.at[0, oz, o - 1],
                x_recv.at[0, oz, o - 1],
                x_peer(o),
            )
            for o in range(1, 4)
        ]
        for oz in order
    }
    for oz in order:
        for copy in along_x[oz]:
            copy.start()
    along_z = []
    for oz in order:
        for copy in along_x[oz]:
            copy.wait_recv()
        where = rows_of(z_index(oz))
        total = term[rows_of(x * 4 + z_index(oz)), :]
        for o in range(3):
            total += part_x[o, where, :]
        piece[where, :] = total
        if oz:
            copy = remote(
                piece.at[where], part_z.at[oz - 1], z_send.at[0, oz - 1], z_recv.at[0, oz - 1], z_peer(oz)
            )
            copy.start()
            along_z.append(copy)
    for oz in order:
        for copy in along_x[oz]:
            copy.wait_send()
    for o, copy in enumerate(along_z):
        copy.wait()
        total += part_z[o]
    mine = rows_of(z_lo)
    merged[mine, :] = total / lax.axis_size("pos")

    def place(index):
        row = lax.rem(x, 2) * quarter + index * small
        return gradient.at[x // 2, pl.ds(pl.multiple_of(row, small), small)]

    gather_z = [
        remote(merged.at[mine], merged.at[mine], z_send.at[1, o - 1], z_recv.at[1, o - 1], z_peer(o))
        for o in range(1, 4)
    ]
    for copy in gather_z:
        copy.start()
    gather_x, keeps = [], []
    for oz in range(4):
        index = lax.rem(z_lo + 4 - oz, 4)
        if oz:
            gather_z[oz - 1].wait_recv()
        for o in range(1, 4):
            copy = remote(
                merged.at[rows_of(index)], place(index), x_send.at[1, oz, o - 1], x_recv.at[1, oz, o - 1], x_peer(o)
            )
            copy.start()
            gather_x.append(copy)
        keep = pltpu.make_async_copy(merged.at[rows_of(index)], place(index), out_sem.at[1 + oz])
        keep.start()
        keeps.append(keep)
    for copy in gather_x + keeps:
        copy.wait()
    for copy in gather_z:
        copy.wait_send()
    finish.wait()


def local(labels, magnet_mask, reluctivity, rotor_shift, potential, adjoint_load):
    cx, cy = labels.shape[1:]
    tall = cx + 2 * PAD
    floats = lambda *shape: pltpu.VMEM(shape, jnp.float32)
    sems = pltpu.SemaphoreType.DMA
    return pl.pallas_call(
        kernel,
        out_shape=(
            jax.ShapeDtypeStruct(labels.shape, jnp.float32),
            jax.ShapeDtypeStruct(adjoint_load.shape, jnp.float32),
        ),
        in_specs=[pl.BlockSpec(memory_space=pltpu.SMEM)] * 2 + [pl.BlockSpec(memory_space=pltpu.HBM)] * 4,
        out_specs=(pl.BlockSpec(memory_space=pl.ANY),) * 2,
        scratch_shapes=[
            pltpu.VMEM((4, cx, cy), jnp.int32),
            floats(4, tall, cy),
            floats(4, tall, cy),
            floats(4, tall, cy),
            floats(4, tall, cy),
            floats(4, tall, cy),
            pltpu.VMEM((2, cx, cy), jnp.int32),
            floats(2 * cx, cy),
            floats(3, cx // 4, cy),
            floats(2, 8, 128),
            floats(8, 8, 128),
            floats(4, 8, 128),
            floats(3, cx // 2, cy),
            floats(3, cx // 8, cy),
            floats(cx // 2, cy),
            floats(cx // 2, cy),
            sems((4,)),
            sems((4, 3, 4)),
            sems((4, 2, 4)),
            sems((4,)),
            sems((4,)),
            sems((3,)),
            sems((3,)),
            sems((7,)),
            sems((7,)),
            sems((3,)),
            sems((3,)),
            sems((2, 4, 3)),
            sems((2, 4, 3)),
            sems((2, 3)),
            sems((2, 3)),
            sems((5,)),
        ],
        compiler_params=pltpu.CompilerParams(
            collective_id=0, has_side_effects=True, vmem_limit_bytes=24 << 20
        ),
    )(reluctivity, rotor_shift, *[pltpu.with_memory_space_constraint(v, pltpu.HBM) for v in (labels, magnet_mask, potential, adjoint_load)])


def solution(mesh):
    return jax.shard_map(
        local,
        mesh=mesh,
        in_specs=(
            P("slab", None, None),
            P("slab", None, None),
            P(),
            P("pos"),
            P("pos", "slab", None, None),
            P("pos", "slab", None, None),
        ),
        out_specs=(P("slab", None, None), P("pos", "slab", None, None)),
        check_vma=False,
    )
```

```python
import jax
import jax.numpy as jnp
from jax import lax
from jax.experimental import pallas as pl
from jax.experimental.pallas import tpu as pltpu
from jax.sharding import PartitionSpec as P

MESH = pl.DeviceIdType.MESH
PAD = 8
ROWS = 128
diagonal_shift = 0.5


def fold(block):
    half = block.shape[1] // 2
    narrow = block[:, :half] + block[:, half:]
    return narrow.reshape(narrow.shape[0] // 8, 8, half).sum(axis=0)


def kernel(
    reluctivity, shift, labels, mask, potential, load, gradient, adjoint,
    label_x, nu_x, d_x, w_x, a_x, pot_x, mask_x, term, fields, relay, tile, near, far,
    part_x, part_z, piece, merged, local_sem, send_sem, recv_sem, relay_send, relay_recv, share_send, share_recv,
    near_send, near_recv, far_send, far_recv, x_send, x_recv, z_send, z_recv, out_sem,
):
    pos, slab = lax.axis_index("pos"), lax.axis_index("slab")
    n_slab = lax.axis_size("slab")
    up, down = lax.rem(slab + 1, n_slab), lax.rem(slab + n_slab - 1, n_slab)
    z_hi, inner = slab // 8, lax.rem(slab, 8)
    z_lo, x = pos // 4, lax.rem(pos, 4)
    cx, cy = labels.shape[1], labels.shape[2]

    local = [
        pltpu.make_async_copy(source, target, local_sem.at[i])
        for i, (source, target) in enumerate(
            (
                (load.at[0], d_x.at[pl.ds(1, 2), pl.ds(PAD, cx)]),
                (labels, label_x.at[pl.ds(1, 2)]),
                (potential.at[0], pot_x.at[pl.ds(1, 2), pl.ds(PAD, cx)]),
                (mask, mask_x),
            )
        )
    ]
    for copy in local:
        copy.start()

    def near_peer(o):
        return {"slab": z_hi * 8 + lax.rem(inner + o, 8)}

    def far_peer(o):
        return {"slab": lax.rem(z_hi + o, 4) * 8 + inner}

    def x_index(o):
        return lax.rem(x + o, 4)

    def z_index(o):
        return lax.rem(z_lo + o, 4)

    peers = [{"slab": up}, {"slab": down}]
    peers += [near_peer(o) for o in range(1, 8)]
    peers += [far_peer(o) for o in range(1, 4)]
    peers += [{"pos": z_lo * 4 + x_index(o)} for o in range(1, 4)]
    peers += [{"pos": z_index(o) * 4 + x} for o in range(1, 4)]
    barrier = pltpu.get_barrier_semaphore()

    def greet(peer):
        pl.semaphore_signal(barrier, inc=1, device_id=peer, device_id_type=MESH)

    z_up, z_down = lax.rem(z_hi + 1, 4) * 8, lax.rem(z_hi + 3, 4) * 8
    is_first, is_last = inner == 0, inner == 7
    odd = lax.rem(inner, 2) == 1
    is_up_relay = jnp.logical_and(odd, inner < 7)
    is_down_relay = jnp.logical_and(jnp.logical_not(odd), inner > 0)
    for peer in peers:
        greet(peer)

    @pl.when(is_first)
    def _():
        for i in (1, 3, 5):
            greet({"slab": z_down + i})

    @pl.when(is_last)
    def _():
        for i in (2, 4, 6):
            greet({"slab": z_up + i})

    @pl.when(is_up_relay)
    def _():
        greet({"slab": z_up})

    @pl.when(is_down_relay)
    def _():
        greet({"slab": z_down + 7})

    ends = jnp.logical_or(is_first, is_last)
    pl.semaphore_wait(barrier, len(peers) + jnp.where(ends, 3, 1))
    strip = cx // 4
    row = inner // 2

    def part(side, k):
        if k == 3 - 3 * side:
            return pl.ds(0 if side else 3 * strip, cx - 3 * strip)
        return pl.ds(k * strip + side * (cx - 4 * strip), strip)

    class Halo:
        def __init__(self, which, first, last, target, buffer):
            def send(source, where, peer, side, k):
                return pltpu.make_async_remote_copy(
                    src_ref=source,
                    dst_ref=where,
                    send_sem=send_sem.at[which, side, k],
                    recv_sem=recv_sem.at[which, side, k],
                    device_id={"slab": peer},
                    device_id_type=MESH,
                )

            def through(source, side, k, peer):
                return pltpu.make_async_remote_copy(
                    src_ref=source.at[part(side, k)],
                    dst_ref=buffer,
                    send_sem=send_sem.at[which, 2, k],
                    recv_sem=relay_recv.at[which],
                    device_id={"slab": peer},
                    device_id_type=MESH,
                )

            def forward(side, ghost, peer):
                first = row * strip + side * (cx - 4 * strip)
                where = pl.ds(pl.multiple_of(first, PAD), strip)
                return pltpu.make_async_remote_copy(
                    src_ref=buffer,
                    dst_ref=target(ghost).at[where],
                    send_sem=relay_send.at[which],
                    recv_sem=recv_sem.at[which, side, row],
                    device_id={"slab": peer},
                    device_id_type=MESH,
                )

            def pieces(source, side, ghost, peer):
                return [
                    send(
                        source.at[part(side, k)],
                        target(ghost).at[part(side, k)],
                        peer, side, k,
                    )
                    for k in range(4)
                ]

            self.whole = [
                (send(last, target(0), up, 0, 0), is_last, is_first),
                (send(first, target(3), down, 1, 0), is_first, is_last),
            ]
            self.parts = [pieces(last, 0, 0, up), pieces(first, 1, 3, down)]
            self.through = [
                [through(last, 0, k, z_hi * 8 + 2 * k + 1) for k in (0, 1, 2)],
                [through(first, 1, k, z_hi * 8 + 2 * k) for k in (1, 2, 3)],
            ]
            self.forward = [
                (is_up_relay, forward(0, 0, z_up)),
                (is_down_relay, forward(1, 3, z_down + 7)),
            ]
            self.arrive = through(last, 0, 0, z_hi * 8)

        def start(self):
            for side, (copy, leaves, _) in enumerate(self.whole):
                direct = self.parts[side][3 - 3 * side]

                @pl.when(leaves)
                def _():
                    for piece in self.through[side]:
                        piece.start()
                    direct.start()

                @pl.when(jnp.logical_not(leaves))
                def _():
                    copy.start()

        def relay(self):
            for role, copy in self.forward:

                @pl.when(role)
                def _():
                    self.arrive.wait_recv()
                    copy.start()

        def wait(self):
            for side, (copy, leaves, enters) in enumerate(self.whole):
                direct = self.parts[side][3 - 3 * side]

                @pl.when(enters)
                def _():
                    for piece in self.parts[side]:
                        piece.wait_recv()

                @pl.when(jnp.logical_not(enters))
                def _():
                    copy.wait_recv()

                @pl.when(leaves)
                def _():
                    for piece in self.through[side]:
                        piece.wait_send()
                    direct.wait_send()

                @pl.when(jnp.logical_not(leaves))
                def _():
                    copy.wait_send()

            for role, copy in self.forward:

                @pl.when(role)
                def _():
                    copy.wait_send()

    class Shared:
        def __init__(self, which, first, last, target):
            def send(source, where, peer, side):
                return pltpu.make_async_remote_copy(
                    src_ref=source,
                    dst_ref=where,
                    send_sem=send_sem.at[which, side, 0],
                    recv_sem=recv_sem.at[which, side, 0],
                    device_id={"slab": peer},
                    device_id_type=MESH,
                )

            quarter = pl.ds(pl.multiple_of(x * strip, strip), strip)

            def share(ghost, o):
                return pltpu.make_async_remote_copy(
                    src_ref=target(ghost).at[quarter],
                    dst_ref=target(ghost).at[quarter],
                    send_sem=share_send.at[o - 1],
                    recv_sem=share_recv.at[o - 1],
                    device_id={"pos": z_lo * 4 + x_index(o)},
                    device_id_type=MESH,
                )

            self.sides = [
                (
                    send(source, target(ghost), peer, side),
                    send(source.at[quarter], target(ghost).at[quarter], peer, side),
                    [share(ghost, o) for o in range(1, 4)],
                    leaves,
                    enters,
                )
                for side, (source, ghost, peer, leaves, enters) in enumerate(
                    ((last, 0, up, is_last, is_first), (first, 3, down, is_first, is_last))
                )
            ]

        def start(self):
            for whole, quarter, _, leaves, _ in self.sides:

                @pl.when(leaves)
                def _():
                    quarter.start()

                @pl.when(jnp.logical_not(leaves))
                def _():
                    whole.start()

        def relay(self):
            for _, quarter, shares, _, enters in self.sides:

                @pl.when(enters)
                def _():
                    quarter.wait_recv()
                    for share in shares:
                        share.start()

        def wait(self):
            for whole, quarter, shares, leaves, enters in self.sides:

                @pl.when(enters)
                def _():
                    for share in shares:
                        share.wait()

                @pl.when(jnp.logical_not(enters))
                def _():
                    whole.wait_recv()

                @pl.when(leaves)
                def _():
                    quarter.wait_send()

                @pl.when(jnp.logical_not(leaves))
                def _():
                    whole.wait_send()

    def padded(ref):
        return lambda layer: ref.at[layer, pl.ds(PAD, cx)]

    d_halo = Halo(0, load.at[0, 0], load.at[0, 1], padded(d_x), relay.at[0])
    label_halo = Shared(1, labels.at[0], labels.at[1], lambda layer: label_x.at[layer])
    pot_halo = Halo(2, potential.at[0, 0], potential.at[0, 1], padded(pot_x), relay.at[1])
    w_halo = Halo(3, padded(w_x)(1), padded(w_x)(2), padded(w_x), relay.at[2])
    label_halo.start()
    d_halo.start()

    for ref in (nu_x, d_x, w_x, pot_x):
        for layer in (1, 2):
            ref[layer, pl.ds(0, PAD), :] = jnp.zeros((PAD, cy), jnp.float32)
            ref[layer, pl.ds(PAD + cx, PAD), :] = jnp.zeros((PAD, cy), jnp.float32)

    low = jnp.where(slab > 0, 1.0, 0.0)
    high = jnp.where(slab < n_slab - 1, 1.0, 0.0)
    live = (low, 1.0, 1.0, high)
    table = [reluctivity[i] for i in range(4)]
    offset = shift[0]

    def materials(layers):
        def lookup(index):
            result = jnp.where(index == 1, table[1], table[0])
            result = jnp.where(index == 2, table[2], result)
            return jnp.where(index == 3, table[3], result)

        @pl.loop(0, cx // 2 // ROWS)
        def _(i):
            r = pl.multiple_of(i * ROWS, ROWS)
            s = pl.multiple_of(i * ROWS + cx // 2, ROWS)
            for layer in layers:
                turned = pltpu.roll(lookup(label_x[layer, pl.ds(r, ROWS), :]), offset, 1)
                nu_x[layer, pl.ds(PAD + r, ROWS), :] = turned * live[layer]
                still = lookup(label_x[layer, pl.ds(s, ROWS), :])
                nu_x[layer, pl.ds(PAD + s, ROWS), :] = still * live[layer]

    def at(ref, layer, r):
        return ref[layer, pl.ds(PAD + r, ROWS), :]

    def tall(ref, layer, r):
        return ref[layer, pl.ds(r, ROWS + 2 * PAD), :]

    def middle(block):
        return block[PAD : PAD + ROWS]

    def before(block):
        return pltpu.roll(block, 1, 0)

    def after(block):
        return pltpu.roll(block, ROWS + 2 * PAD - 1, 0)

    def operator(ref, layer, r, below, above):
        v_tall, nu_tall = tall(ref, layer, r), tall(nu_x, layer, r)
        flux = 0.5 * (nu_tall + after(nu_tall)) * (v_tall - after(v_tall))
        v, nu = middle(v_tall), middle(nu_tall)
        result = diagonal_shift * v + middle(flux - before(flux))
        for step, other in ((-1, below), (1, above)):
            if other is not None:
                result += 0.5 * (nu + at(nu_x, layer + step, r)) * (v - other)
        flux = 0.5 * (nu + pltpu.roll(nu, cy - 1, 1)) * (v - pltpu.roll(v, cy - 1, 1))
        return v, result + (flux - pltpu.roll(flux, 1, 1))

    zero = jnp.zeros((8, cy // 2), jnp.float32)

    local[1].wait()
    materials((1, 2))
    local[0].wait()

    @pl.loop(0, cx // ROWS)
    def _(i):
        r = pl.multiple_of(i * ROWS, ROWS)
        for layer, others in ((1, (None, at(d_x, 2, r))), (2, (at(d_x, 1, r), None))):
            _, image = operator(d_x, layer, r, *others)
            w_x[layer, pl.ds(PAD + r, ROWS), :] = image

    w_halo.start()
    pot_halo.start()
    label_halo.relay()
    d_halo.relay()
    w_halo.relay()
    pot_halo.relay()
    label_halo.wait()
    materials((0, 3))
    d_halo.wait()
    w_halo.wait()

    def sides(ref, layer, r):
        below, above = at(ref, layer - 1, r), at(ref, layer + 1, r)
        return (below * low, above) if layer == 1 else (below, above * high)

    def first_pass(i, sums):
        norm, energy = sums
        r = pl.multiple_of(i * ROWS, ROWS)
        for layer, ghost, exists in ((1, 0, low), (2, 3, high)):
            d = at(d_x, layer, r)
            nu = at(nu_x, layer, r) + at(nu_x, ghost, r)
            flux = 0.5 * nu * (d - at(d_x, ghost, r) * exists)
            image = at(w_x, layer, r) + flux
            w_x[layer, pl.ds(PAD + r, ROWS), :] = image
            w_x[ghost, pl.ds(PAD + r, ROWS), :] = at(w_x, ghost, r) - flux
            norm += fold(d * d)
            energy += fold(d * image)
        return norm, energy

    sums = lax.fori_loop(0, cx // ROWS, first_pass, (zero, zero))

    def whole_sum(part):
        return jnp.sum(jnp.sum(part, axis=0, keepdims=True), axis=1, keepdims=True)

    def wide(value, width=cy):
        return jnp.broadcast_to(value[:, :1], (1, width))

    def quotient(top, bottom):
        some = bottom > 0.0
        return jnp.where(some, top / jnp.where(some, bottom, 1.0), 0.0)

    norm, energy = [whole_sum(part) for part in sums]
    theta = quotient(energy, norm)
    theta_wide = wide(theta)
    def second_pass(i, sums):
        m1, m2, m3, m4 = sums
        r = pl.multiple_of(i * ROWS, ROWS)
        for layer in (1, 2):
            w, image = operator(w_x, layer, r, *sides(w_x, layer, r))
            d = at(d_x, layer, r)
            u = w - theta_wide * d
            q = image - theta_wide * w
            m1 += fold(d * u)
            m2 += fold(u * u)
            m3 += fold(u * q)
            m4 += fold(d * q)
        return m1, m2, m3, m4

    sums = lax.fori_loop(0, cx // ROWS, second_pass, (zero,) * 4)

    def combine(box):
        th, m0, m1, m2, m3, m4 = [box[:, i, :] for i in range(6)]
        total = lambda value: jnp.sum(value, axis=0, keepdims=True)
        centre = quotient(total(th * m0 + m1), total(m0))
        e = centre - th
        dw = m1 + th * m0
        return (
            centre,
            total(m0),
            total(m1 - e * m0),
            total(m2 - e * (2.0 * m1 - e * m0)),
            total(m3 - e * (m2 + th * m1 + m4 - e * dw)),
            total(m4 - e * dw),
        )

    def exchange(stage, values, size, mine, box, peer, send, recv):
        for i, value in enumerate(values):
            tile[stage, pl.ds(i, 1), :] = wide(value, tile.shape[2])
        copies = [
            pltpu.make_async_remote_copy(
                src_ref=tile.at[stage],
                dst_ref=box.at[mine],
                send_sem=send.at[o - 1],
                recv_sem=recv.at[o - 1],
                device_id=peer(o),
                device_id_type=MESH,
            )
            for o in range(1, size)
        ]
        for copy in copies:
            copy.start()
        box[mine] = tile[stage]

        def finish():
            for copy in copies:
                copy.wait()
            return combine(box)

        return finish

    values = (theta, norm, *[whole_sum(part) for part in sums])
    values = exchange(0, values, 8, inner, near, near_peer, near_send, near_recv)()
    arrive = exchange(1, values, 4, z_hi, far, far_peer, far_send, far_recv)
    local[2].wait()
    local[3].wait()
    pot_halo.wait()

    def slopes(ref, layer, r):
        below, above = sides(ref, layer, r)
        v_tall = tall(ref, layer, r)
        v = middle(v_tall)
        return (
            above - below,
            middle(after(v_tall) - before(v_tall)),
            pltpu.roll(v, cy - 1, 1) - pltpu.roll(v, 1, 1),
        )

    @pl.loop(0, cx // ROWS)
    def _(i):
        r = pl.multiple_of(i * ROWS, ROWS)
        for layer in (1, 2):
            chosen = mask_x[layer - 1, pl.ds(r, ROWS), :].astype(jnp.float32)
            weight = 0.25 * chosen * at(nu_x, layer, r)
            pot = slopes(pot_x, layer, r)
            where = pl.ds((layer - 1) * cx + r, ROWS)
            for index, ref in enumerate((d_x, w_x)):
                other = slopes(ref, layer, r)
                fields[index, where, :] = weight * sum(p * q for p, q in zip(pot, other))
            fields[2, where, :] = 0.5 * weight * sum(p * p for p in pot)

    values = arrive()
    centre, m0, _, m2, m3, _ = values
    alpha0 = 1.0 / centre
    beta = alpha0 * alpha0 * m2 / m0
    alpha1 = m2 / (m3 - alpha0 * m2 * (m2 / m0))
    from_d = wide(alpha0 + alpha1 * (1.0 + beta))
    from_w = wide(alpha0 * alpha1)

    @pl.loop(0, 2 * cx // ROWS)
    def _(i):
        rows = pl.ds(pl.multiple_of(i * ROWS, ROWS), ROWS)
        term[rows, :] = from_d * fields[0, rows, :] - from_w * fields[1, rows, :] + fields[2, rows, :]

    quarter, small = 2 * cx // 4, 2 * cx // 16

    def x_peer(o):
        return {"pos": z_lo * 4 + x_index(o)}

    def z_peer(o):
        return {"pos": z_index(o) * 4 + x}

    def remote(source, target, send, recv, peer):
        return pltpu.make_async_remote_copy(
            src_ref=source, dst_ref=target, send_sem=send, recv_sem=recv, device_id=peer, device_id_type=MESH
        )

    def rows_of(index):
        return pl.ds(pl.multiple_of(index * small, small), small)

    order = (1, 2, 3, 0)
    along_x = {
        oz: [
            remote(
                term.at[rows_of(x_index(o) * 4 + z_index(oz))],
                part_x.at[o - 1, rows_of(z_index(oz))],
                x_send.at[0, oz, o - 1],
                x_recv.at[0, oz, o - 1],
                x_peer(o),
            )
            for o in range(1, 4)
        ]
        for oz in order
    }
    for oz in order:
        for copy in along_x[oz]:
            copy.start()

    @pl.loop(0, cx // ROWS)
    def _(i):
        r = pl.multiple_of(i * ROWS, ROWS)
        for layer in (1, 2):
            value = from_d * at(d_x, layer, r) - from_w * at(w_x, layer, r)
            a_x[layer - 1, pl.ds(r, ROWS), :] = value

    finish = pltpu.make_async_copy(a_x, adjoint.at[0], out_sem.at[0])
    finish.start()
    along_z = []
    for oz in order:
        for copy in along_x[oz]:
            copy.wait_recv()
        where = rows_of(z_index(oz))
        total = term[rows_of(x * 4 + z_index(oz)), :]
        for o in range(3):
            total += part_x[o, where, :]
        piece[where, :] = total
        if oz:
            copy = remote(
                piece.at[where], part_z.at[oz - 1], z_send.at[0, oz - 1], z_recv.at[0, oz - 1], z_peer(oz)
            )
            copy.start()
            along_z.append(copy)
    for oz in order:
        for copy in along_x[oz]:
            copy.wait_send()
    for o, copy in enumerate(along_z):
        copy.wait()
        total += part_z[o]
    mine = rows_of(z_lo)
    merged[mine, :] = total / lax.axis_size("pos")

    def place(index):
        row = lax.rem(x, 2) * quarter + index * small
        return gradient.at[x // 2, pl.ds(pl.multiple_of(row, small), small)]

    gather_z = [
        remote(merged.at[mine], merged.at[mine], z_send.at[1, o - 1], z_recv.at[1, o - 1], z_peer(o))
        for o in range(1, 4)
    ]
    for copy in gather_z:
        copy.start()
    gather_x, keeps = [], []
    for oz in range(4):
        index = lax.rem(z_lo + 4 - oz, 4)
        if oz:
            gather_z[oz - 1].wait_recv()
        for o in range(1, 4):
            copy = remote(
                merged.at[rows_of(index)], place(index), x_send.at[1, oz, o - 1], x_recv.at[1, oz, o - 1], x_peer(o)
            )
            copy.start()
            gather_x.append(copy)
        keep = pltpu.make_async_copy(merged.at[rows_of(index)], place(index), out_sem.at[1 + oz])
        keep.start()
        keeps.append(keep)
    for copy in gather_x + keeps:
        copy.wait()
    for copy in gather_z:
        copy.wait_send()
    finish.wait()


def local(labels, magnet_mask, reluctivity, rotor_shift, potential, adjoint_load):
    cx, cy = labels.shape[1:]
    tall = cx + 2 * PAD
    floats = lambda *shape: pltpu.VMEM(shape, jnp.float32)
    sems = pltpu.SemaphoreType.DMA
    return pl.pallas_call(
        kernel,
        out_shape=(
            jax.ShapeDtypeStruct(labels.shape, jnp.float32),
            jax.ShapeDtypeStruct(adjoint_load.shape, jnp.float32),
        ),
        in_specs=[pl.BlockSpec(memory_space=pltpu.SMEM)] * 2 + [pl.BlockSpec(memory_space=pltpu.HBM)] * 4,
        out_specs=(pl.BlockSpec(memory_space=pl.ANY),) * 2,
        scratch_shapes=[
            pltpu.VMEM((4, cx, cy), jnp.int32),
            floats(4, tall, cy),
            floats(4, tall, cy),
            floats(4, tall, cy),
            floats(2, cx, cy),
            floats(4, tall, cy),
            pltpu.VMEM((2, cx, cy), jnp.int32),
            floats(2 * cx, cy),
            floats(3, 2 * cx, cy),
            floats(3, cx // 4, cy),
            floats(2, 8, 128),
            floats(8, 8, 128),
            floats(4, 8, 128),
            floats(3, cx // 2, cy),
            floats(3, cx // 8, cy),
            floats(cx // 2, cy),
            floats(cx // 2, cy),
            sems((4,)),
            sems((4, 3, 4)),
            sems((4, 2, 4)),
            sems((4,)),
            sems((4,)),
            sems((3,)),
            sems((3,)),
            sems((7,)),
            sems((7,)),
            sems((3,)),
            sems((3,)),
            sems((2, 4, 3)),
            sems((2, 4, 3)),
            sems((2, 3)),
            sems((2, 3)),
            sems((5,)),
        ],
        compiler_params=pltpu.CompilerParams(
            collective_id=0, has_side_effects=True, vmem_limit_bytes=24 << 20
        ),
    )(reluctivity, rotor_shift, *[pltpu.with_memory_space_constraint(v, pltpu.HBM) for v in (labels, magnet_mask, potential, adjoint_load)])


def solution(mesh):
    return jax.shard_map(
        local,
        mesh=mesh,
        in_specs=(
            P("slab", None, None),
            P("slab", None, None),
            P(),
            P("pos"),
            P("pos", "slab", None, None),
            P("pos", "slab", None, None),
        ),
        out_specs=(P("slab", None, None), P("pos", "slab", None, None)),
        check_vma=False,
    )
```

```python
import jax
import jax.numpy as jnp
from jax import lax
from jax.experimental import pallas as pl
from jax.experimental.pallas import tpu as pltpu
from jax.sharding import PartitionSpec as P

MESH = pl.DeviceIdType.MESH
PAD = 8
ROWS = 128
diagonal_shift = 0.5


def fold(block):
    half = block.shape[1] // 2
    narrow = block[:, :half] + block[:, half:]
    return narrow.reshape(narrow.shape[0] // 8, 8, half).sum(axis=0)


def kernel(
    reluctivity, shift, labels, mask, potential, load, gradient, adjoint,
    label_x, nu_x, d_x, w_x, a_x, pot_x, mask_x, term, fields, relay, tile, box,
    part_x, part_z, piece, merged, local_sem, send_sem, recv_sem, relay_send, relay_recv, share_send, share_recv,
    all_send, all_recv, x_send, x_recv, z_send, z_recv, out_sem,
):
    pos, slab = lax.axis_index("pos"), lax.axis_index("slab")
    n_slab = lax.axis_size("slab")
    up, down = lax.rem(slab + 1, n_slab), lax.rem(slab + n_slab - 1, n_slab)
    z_hi, inner = slab // 8, lax.rem(slab, 8)
    z_lo, x = pos // 4, lax.rem(pos, 4)
    cx, cy = labels.shape[1], labels.shape[2]

    local = [
        pltpu.make_async_copy(source, target, local_sem.at[i])
        for i, (source, target) in enumerate(
            (
                (load.at[0], d_x.at[pl.ds(1, 2), pl.ds(PAD, cx)]),
                (labels, label_x.at[pl.ds(1, 2)]),
                (potential.at[0], pot_x.at[pl.ds(1, 2), pl.ds(PAD, cx)]),
                (mask, mask_x),
            )
        )
    ]
    for copy in local:
        copy.start()

    offsets = [8 * o + i for o in (2, 1, 3) for i in range(8)] + list(range(1, 8))
    members = [{"slab": lax.rem(z_hi + c // 8, 4) * 8 + lax.rem(inner + c % 8, 8)} for c in offsets]

    def x_index(o):
        return lax.rem(x + o, 4)

    def z_index(o):
        return lax.rem(z_lo + o, 4)

    peers = list(members)
    peers += [{"pos": z_lo * 4 + x_index(o)} for o in range(1, 4)]
    peers += [{"pos": z_index(o) * 4 + x} for o in range(1, 4)]
    barrier = pltpu.get_barrier_semaphore()

    def greet(peer):
        pl.semaphore_signal(barrier, inc=1, device_id=peer, device_id_type=MESH)

    z_up, z_down = lax.rem(z_hi + 1, 4) * 8, lax.rem(z_hi + 3, 4) * 8
    is_first, is_last = inner == 0, inner == 7
    odd = lax.rem(inner, 2) == 1
    is_up_relay = jnp.logical_and(odd, inner < 7)
    is_down_relay = jnp.logical_and(jnp.logical_not(odd), inner > 0)
    for peer in peers:
        greet(peer)

    pl.semaphore_wait(barrier, len(peers))
    strip = cx // 4
    row = inner // 2

    def part(side, k):
        if k == 3 - 3 * side:
            return pl.ds(0 if side else 3 * strip, cx - 3 * strip)
        return pl.ds(k * strip + side * (cx - 4 * strip), strip)

    class Halo:
        def __init__(self, which, first, last, target, buffer):
            def send(source, where, peer, side, k):
                return pltpu.make_async_remote_copy(
                    src_ref=source,
                    dst_ref=where,
                    send_sem=send_sem.at[which, side, k],
                    recv_sem=recv_sem.at[which, side, k],
                    device_id={"slab": peer},
                    device_id_type=MESH,
                )

            def through(source, side, k, peer):
                return pltpu.make_async_remote_copy(
                    src_ref=source.at[part(side, k)],
                    dst_ref=buffer,
                    send_sem=send_sem.at[which, 2, k],
                    recv_sem=relay_recv.at[which],
                    device_id={"slab": peer},
                    device_id_type=MESH,
                )

            def forward(side, ghost, peer):
                first = row * strip + side * (cx - 4 * strip)
                where = pl.ds(pl.multiple_of(first, PAD), strip)
                return pltpu.make_async_remote_copy(
                    src_ref=buffer,
                    dst_ref=target(ghost).at[where],
                    send_sem=relay_send.at[which],
                    recv_sem=recv_sem.at[which, side, row],
                    device_id={"slab": peer},
                    device_id_type=MESH,
                )

            def pieces(source, side, ghost, peer):
                return [
                    send(
                        source.at[part(side, k)],
                        target(ghost).at[part(side, k)],
                        peer, side, k,
                    )
                    for k in range(4)
                ]

            self.whole = [
                (send(last, target(0), up, 0, 0), is_last, is_first),
                (send(first, target(3), down, 1, 0), is_first, is_last),
            ]
            self.parts = [pieces(last, 0, 0, up), pieces(first, 1, 3, down)]
            self.through = [
                [through(last, 0, k, z_hi * 8 + 2 * k + 1) for k in (0, 1, 2)],
                [through(first, 1, k, z_hi * 8 + 2 * k) for k in (1, 2, 3)],
            ]
            self.forward = [
                (is_up_relay, forward(0, 0, z_up)),
                (is_down_relay, forward(1, 3, z_down + 7)),
            ]
            self.arrive = through(last, 0, 0, z_hi * 8)

        def start(self):
            for side, (copy, leaves, _) in enumerate(self.whole):
                direct = self.parts[side][3 - 3 * side]

                @pl.when(leaves)
                def _():
                    for piece in self.through[side]:
                        piece.start()
                    direct.start()

                @pl.when(jnp.logical_not(leaves))
                def _():
                    copy.start()

        def relay(self):
            for role, copy in self.forward:

                @pl.when(role)
                def _():
                    self.arrive.wait_recv()
                    copy.start()

        def wait(self):
            for side, (copy, leaves, enters) in enumerate(self.whole):
                direct = self.parts[side][3 - 3 * side]

                @pl.when(enters)
                def _():
                    for piece in self.parts[side]:
                        piece.wait_recv()

                @pl.when(jnp.logical_not(enters))
                def _():
                    copy.wait_recv()

                @pl.when(leaves)
                def _():
                    for piece in self.through[side]:
                        piece.wait_send()
                    direct.wait_send()

                @pl.when(jnp.logical_not(leaves))
                def _():
                    copy.wait_send()

            for role, copy in self.forward:

                @pl.when(role)
                def _():
                    copy.wait_send()

    class Shared:
        def __init__(self, which, first, last, target):
            def send(source, where, peer, side):
                return pltpu.make_async_remote_copy(
                    src_ref=source,
                    dst_ref=where,
                    send_sem=send_sem.at[which, side, 0],
                    recv_sem=recv_sem.at[which, side, 0],
                    device_id={"slab": peer},
                    device_id_type=MESH,
                )

            quarter = pl.ds(pl.multiple_of(x * strip, strip), strip)

            def share(ghost, o):
                return pltpu.make_async_remote_copy(
                    src_ref=target(ghost).at[quarter],
                    dst_ref=target(ghost).at[quarter],
                    send_sem=share_send.at[o - 1],
                    recv_sem=share_recv.at[o - 1],
                    device_id={"pos": z_lo * 4 + x_index(o)},
                    device_id_type=MESH,
                )

            self.sides = [
                (
                    send(source, target(ghost), peer, side),
                    send(source.at[quarter], target(ghost).at[quarter], peer, side),
                    [share(ghost, o) for o in range(1, 4)],
                    leaves,
                    enters,
                )
                for side, (source, ghost, peer, leaves, enters) in enumerate(
                    ((last, 0, up, is_last, is_first), (first, 3, down, is_first, is_last))
                )
            ]

        def start(self):
            for whole, quarter, _, leaves, _ in self.sides:

                @pl.when(leaves)
                def _():
                    quarter.start()

                @pl.when(jnp.logical_not(leaves))
                def _():
                    whole.start()

        def relay(self):
            for _, quarter, shares, _, enters in self.sides:

                @pl.when(enters)
                def _():
                    quarter.wait_recv()
                    for share in shares:
                        share.start()

        def wait(self):
            for whole, quarter, shares, leaves, enters in self.sides:

                @pl.when(enters)
                def _():
                    for share in shares:
                        share.wait()

                @pl.when(jnp.logical_not(enters))
                def _():
                    whole.wait_recv()

                @pl.when(leaves)
                def _():
                    quarter.wait_send()

                @pl.when(jnp.logical_not(leaves))
                def _():
                    whole.wait_send()

    def padded(ref):
        return lambda layer: ref.at[layer, pl.ds(PAD, cx)]

    d_halo = Halo(0, load.at[0, 0], load.at[0, 1], padded(d_x), relay.at[0])
    label_halo = Shared(1, labels.at[0], labels.at[1], lambda layer: label_x.at[layer])
    pot_halo = Halo(2, potential.at[0, 0], potential.at[0, 1], padded(pot_x), relay.at[1])
    w_halo = Halo(3, padded(w_x)(1), padded(w_x)(2), padded(w_x), relay.at[2])
    label_halo.start()
    d_halo.start()

    for ref in (nu_x, d_x, w_x, pot_x):
        for layer in (1, 2):
            ref[layer, pl.ds(0, PAD), :] = jnp.zeros((PAD, cy), jnp.float32)
            ref[layer, pl.ds(PAD + cx, PAD), :] = jnp.zeros((PAD, cy), jnp.float32)

    low = jnp.where(slab > 0, 1.0, 0.0)
    high = jnp.where(slab < n_slab - 1, 1.0, 0.0)
    live = (low, 1.0, 1.0, high)
    table = [reluctivity[i] for i in range(4)]
    offset = shift[0]

    def materials(layers):
        def lookup(index):
            result = jnp.where(index == 1, table[1], table[0])
            result = jnp.where(index == 2, table[2], result)
            return jnp.where(index == 3, table[3], result)

        @pl.loop(0, cx // 2 // ROWS)
        def _(i):
            r = pl.multiple_of(i * ROWS, ROWS)
            s = pl.multiple_of(i * ROWS + cx // 2, ROWS)
            for layer in layers:
                turned = pltpu.roll(lookup(label_x[layer, pl.ds(r, ROWS), :]), offset, 1)
                nu_x[layer, pl.ds(PAD + r, ROWS), :] = turned * live[layer]
                still = lookup(label_x[layer, pl.ds(s, ROWS), :])
                nu_x[layer, pl.ds(PAD + s, ROWS), :] = still * live[layer]

    def at(ref, layer, r):
        return ref[layer, pl.ds(PAD + r, ROWS), :]

    def tall(ref, layer, r):
        return ref[layer, pl.ds(r, ROWS + 2 * PAD), :]

    def middle(block):
        return block[PAD : PAD + ROWS]

    def before(block):
        return pltpu.roll(block, 1, 0)

    def after(block):
        return pltpu.roll(block, ROWS + 2 * PAD - 1, 0)

    def operator(ref, layer, r, below, above):
        v_tall, nu_tall = tall(ref, layer, r), tall(nu_x, layer, r)
        flux = 0.5 * (nu_tall + after(nu_tall)) * (v_tall - after(v_tall))
        v, nu = middle(v_tall), middle(nu_tall)
        result = diagonal_shift * v + middle(flux - before(flux))
        for step, other in ((-1, below), (1, above)):
            if other is not None:
                result += 0.5 * (nu + at(nu_x, layer + step, r)) * (v - other)
        flux = 0.5 * (nu + pltpu.roll(nu, cy - 1, 1)) * (v - pltpu.roll(v, cy - 1, 1))
        return v, result + (flux - pltpu.roll(flux, 1, 1))

    zero = jnp.zeros((8, cy // 2), jnp.float32)

    local[1].wait()
    materials((1, 2))
    local[0].wait()

    @pl.loop(0, cx // ROWS)
    def _(i):
        r = pl.multiple_of(i * ROWS, ROWS)
        for layer, others in ((1, (None, at(d_x, 2, r))), (2, (at(d_x, 1, r), None))):
            _, image = operator(d_x, layer, r, *others)
            w_x[layer, pl.ds(PAD + r, ROWS), :] = image

    w_halo.start()
    pot_halo.start()
    label_halo.relay()
    d_halo.relay()
    w_halo.relay()
    pot_halo.relay()
    label_halo.wait()
    materials((0, 3))
    d_halo.wait()
    w_halo.wait()

    def sides(ref, layer, r):
        below, above = at(ref, layer - 1, r), at(ref, layer + 1, r)
        return (below * low, above) if layer == 1 else (below, above * high)

    def first_pass(i, sums):
        norm, energy = sums
        r = pl.multiple_of(i * ROWS, ROWS)
        for layer, ghost, exists in ((1, 0, low), (2, 3, high)):
            d = at(d_x, layer, r)
            nu = at(nu_x, layer, r) + at(nu_x, ghost, r)
            flux = 0.5 * nu * (d - at(d_x, ghost, r) * exists)
            image = at(w_x, layer, r) + flux
            w_x[layer, pl.ds(PAD + r, ROWS), :] = image
            w_x[ghost, pl.ds(PAD + r, ROWS), :] = at(w_x, ghost, r) - flux
            norm += fold(d * d)
            energy += fold(d * image)
        return norm, energy

    sums = lax.fori_loop(0, cx // ROWS, first_pass, (zero, zero))

    def whole_sum(part):
        return jnp.sum(jnp.sum(part, axis=0, keepdims=True), axis=1, keepdims=True)

    def wide(value, width=cy):
        return jnp.broadcast_to(value[:, :1], (1, width))

    def quotient(top, bottom):
        some = bottom > 0.0
        return jnp.where(some, top / jnp.where(some, bottom, 1.0), 0.0)

    norm, energy = [whole_sum(part) for part in sums]
    theta = quotient(energy, norm)
    theta_wide = wide(theta)
    def second_pass(i, sums):
        m1, m2, m3, m4 = sums
        r = pl.multiple_of(i * ROWS, ROWS)
        for layer in (1, 2):
            w, image = operator(w_x, layer, r, *sides(w_x, layer, r))
            d = at(d_x, layer, r)
            u = w - theta_wide * d
            q = image - theta_wide * w
            m1 += fold(d * u)
            m2 += fold(u * u)
            m3 += fold(u * q)
            m4 += fold(d * q)
        return m1, m2, m3, m4

    sums = lax.fori_loop(0, cx // ROWS, second_pass, (zero,) * 4)

    def combine():
        rows = box[:, 0, :]
        width = rows.shape[1]
        th, m0, m1, m2, m3, m4 = [pltpu.roll(rows, (width - i) % width, 1) for i in range(6)]
        total = lambda value: jnp.sum(value, axis=0, keepdims=True)
        centre = quotient(total(th * m0 + m1), total(m0))
        e = centre - th
        dw = m1 + th * m0
        return (
            centre,
            total(m0),
            total(m2 - e * (2.0 * m1 - e * m0)),
            total(m3 - e * (m2 + th * m1 + m4 - e * dw)),
        )

    def exchange(values):
        lane = lax.broadcasted_iota(jnp.int32, (1, tile.shape[1]), 1)
        packed = wide(values[0], tile.shape[1])
        for i, value in enumerate(values[1:], 1):
            packed = jnp.where(lane == i, wide(value, tile.shape[1]), packed)
        line = pl.ds(0, 1)
        tile[line, :] = packed
        copies = [
            pltpu.make_async_remote_copy(
                src_ref=tile.at[line],
                dst_ref=box.at[slab, line],
                send_sem=all_send.at[k],
                recv_sem=all_recv.at[k],
                device_id=peer,
                device_id_type=MESH,
            )
            for k, peer in enumerate(members)
        ]
        for copy in copies:
            copy.start()
        box[slab, line, :] = packed

        def finish():
            for copy in copies:
                copy.wait_recv()
            result = combine()
            return result, copies

        return finish

    values = (theta, norm, *[whole_sum(part) for part in sums])
    arrive = exchange(values)
    local[2].wait()
    local[3].wait()
    pot_halo.wait()

    def slopes(ref, layer, r):
        below, above = sides(ref, layer, r)
        v_tall = tall(ref, layer, r)
        v = middle(v_tall)
        return (
            above - below,
            middle(after(v_tall) - before(v_tall)),
            pltpu.roll(v, cy - 1, 1) - pltpu.roll(v, 1, 1),
        )

    @pl.loop(0, cx // ROWS)
    def _(i):
        r = pl.multiple_of(i * ROWS, ROWS)
        for layer in (1, 2):
            chosen = mask_x[layer - 1, pl.ds(r, ROWS), :].astype(jnp.float32)
            weight = 0.25 * chosen * at(nu_x, layer, r)
            pot = slopes(pot_x, layer, r)
            where = pl.ds((layer - 1) * cx + r, ROWS)
            for index, ref in enumerate((d_x, w_x)):
                other = slopes(ref, layer, r)
                fields[index, where, :] = weight * sum(p * q for p, q in zip(pot, other))
            fields[2, where, :] = 0.5 * weight * sum(p * p for p in pot)

    values, sent = arrive()
    centre, m0, m2, m3 = values
    alpha0 = 1.0 / centre
    beta = alpha0 * alpha0 * m2 / m0
    alpha1 = m2 / (m3 - alpha0 * m2 * (m2 / m0))
    from_d = wide(alpha0 + alpha1 * (1.0 + beta))
    from_w = wide(alpha0 * alpha1)

    @pl.loop(0, 2 * cx // ROWS)
    def _(i):
        rows = pl.ds(pl.multiple_of(i * ROWS, ROWS), ROWS)
        term[rows, :] = from_d * fields[0, rows, :] - from_w * fields[1, rows, :] + fields[2, rows, :]

    quarter, small = 2 * cx // 4, 2 * cx // 16

    def x_peer(o):
        return {"pos": z_lo * 4 + x_index(o)}

    def z_peer(o):
        return {"pos": z_index(o) * 4 + x}

    def remote(source, target, send, recv, peer):
        return pltpu.make_async_remote_copy(
            src_ref=source, dst_ref=target, send_sem=send, recv_sem=recv, device_id=peer, device_id_type=MESH
        )

    def rows_of(index):
        return pl.ds(pl.multiple_of(index * small, small), small)

    order = (1, 2, 3, 0)
    along_x = {
        oz: [
            remote(
                term.at[rows_of(x_index(o) * 4 + z_index(oz))],
                part_x.at[o - 1, rows_of(z_index(oz))],
                x_send.at[0, oz, o - 1],
                x_recv.at[0, oz, o - 1],
                x_peer(o),
            )
            for o in range(1, 4)
        ]
        for oz in order
    }
    for oz in order:
        for copy in along_x[oz]:
            copy.start()

    @pl.loop(0, cx // ROWS)
    def _(i):
        r = pl.multiple_of(i * ROWS, ROWS)
        for layer in (1, 2):
            value = from_d * at(d_x, layer, r) - from_w * at(w_x, layer, r)
            a_x[layer - 1, pl.ds(r, ROWS), :] = value

    finish = pltpu.make_async_copy(a_x, adjoint.at[0], out_sem.at[0])
    finish.start()
    for copy in sent:
        copy.wait_send()
    along_z = []
    for oz in order:
        for copy in along_x[oz]:
            copy.wait_recv()
        where = rows_of(z_index(oz))
        total = term[rows_of(x * 4 + z_index(oz)), :]
        for o in range(3):
            total += part_x[o, where, :]
        piece[where, :] = total
        if oz:
            copy = remote(
                piece.at[where], part_z.at[oz - 1], z_send.at[0, oz - 1], z_recv.at[0, oz - 1], z_peer(oz)
            )
            copy.start()
            along_z.append(copy)
    for oz in order:
        for copy in along_x[oz]:
            copy.wait_send()
    for o, copy in enumerate(along_z):
        copy.wait()
        total += part_z[o]
    mine = rows_of(z_lo)
    merged[mine, :] = total / lax.axis_size("pos")

    def place(index):
        row = lax.rem(x, 2) * quarter + index * small
        return gradient.at[x // 2, pl.ds(pl.multiple_of(row, small), small)]

    gather_z = [
        remote(merged.at[mine], merged.at[mine], z_send.at[1, o - 1], z_recv.at[1, o - 1], z_peer(o))
        for o in range(1, 4)
    ]
    for copy in gather_z:
        copy.start()
    gather_x, keeps = [], []
    for oz in range(4):
        index = lax.rem(z_lo + 4 - oz, 4)
        if oz:
            gather_z[oz - 1].wait_recv()
        for o in range(1, 4):
            copy = remote(
                merged.at[rows_of(index)], place(index), x_send.at[1, oz, o - 1], x_recv.at[1, oz, o - 1], x_peer(o)
            )
            copy.start()
            gather_x.append(copy)
        keep = pltpu.make_async_copy(merged.at[rows_of(index)], place(index), out_sem.at[1 + oz])
        keep.start()
        keeps.append(keep)
    for copy in gather_x + keeps:
        copy.wait()
    for copy in gather_z:
        copy.wait_send()
    finish.wait()


def local(labels, magnet_mask, reluctivity, rotor_shift, potential, adjoint_load):
    cx, cy = labels.shape[1:]
    tall = cx + 2 * PAD
    floats = lambda *shape: pltpu.VMEM(shape, jnp.float32)
    sems = pltpu.SemaphoreType.DMA
    return pl.pallas_call(
        kernel,
        out_shape=(
            jax.ShapeDtypeStruct(labels.shape, jnp.float32),
            jax.ShapeDtypeStruct(adjoint_load.shape, jnp.float32),
        ),
        in_specs=[pl.BlockSpec(memory_space=pltpu.SMEM)] * 2 + [pl.BlockSpec(memory_space=pltpu.HBM)] * 4,
        out_specs=(pl.BlockSpec(memory_space=pl.ANY),) * 2,
        scratch_shapes=[
            pltpu.VMEM((4, cx, cy), jnp.int32),
            floats(4, tall, cy),
            floats(4, tall, cy),
            floats(4, tall, cy),
            floats(2, cx, cy),
            floats(4, tall, cy),
            pltpu.VMEM((2, cx, cy), jnp.int32),
            floats(2 * cx, cy),
            floats(3, 2 * cx, cy),
            floats(3, cx // 4, cy),
            floats(8, 128),
            floats(32, 8, 128),
            floats(3, cx // 2, cy),
            floats(3, cx // 8, cy),
            floats(cx // 2, cy),
            floats(cx // 2, cy),
            sems((4,)),
            sems((4, 3, 4)),
            sems((4, 2, 4)),
            sems((4,)),
            sems((4,)),
            sems((3,)),
            sems((3,)),
            sems((31,)),
            sems((31,)),
            sems((2, 4, 3)),
            sems((2, 4, 3)),
            sems((2, 3)),
            sems((2, 3)),
            sems((5,)),
        ],
        compiler_params=pltpu.CompilerParams(
            collective_id=0, has_side_effects=True, vmem_limit_bytes=24 << 20
        ),
    )(reluctivity, rotor_shift, *[pltpu.with_memory_space_constraint(v, pltpu.HBM) for v in (labels, magnet_mask, potential, adjoint_load)])


def solution(mesh):
    return jax.shard_map(
        local,
        mesh=mesh,
        in_specs=(
            P("slab", None, None),
            P("slab", None, None),
            P(),
            P("pos"),
            P("pos", "slab", None, None),
            P("pos", "slab", None, None),
        ),
        out_specs=(P("slab", None, None), P("pos", "slab", None, None)),
        check_vma=False,
    )
```

```python
import jax
import jax.numpy as jnp
from jax import lax
from jax.experimental import pallas as pl
from jax.experimental.pallas import tpu as pltpu
from jax.sharding import PartitionSpec as P

MESH = pl.DeviceIdType.MESH
PAD = 8
ROWS = 128
diagonal_shift = 0.5


def fold(block):
    half = block.shape[1] // 2
    narrow = block[:, :half] + block[:, half:]
    return narrow.reshape(narrow.shape[0] // 8, 8, half).sum(axis=0)


def kernel(
    reluctivity, shift, labels, mask, potential, load, gradient, adjoint,
    label_x, nu_x, d_x, w_x, a_x, pot_x, mask_x, term, fields, relay, tile, box,
    part_x, part_z, piece, merged, local_sem, send_sem, recv_sem, relay_send, relay_recv, share_send, share_recv,
    all_send, all_recv, x_send, x_recv, z_send, z_recv, out_sem,
):
    pos, slab = lax.axis_index("pos"), lax.axis_index("slab")
    n_slab = lax.axis_size("slab")
    up, down = lax.rem(slab + 1, n_slab), lax.rem(slab + n_slab - 1, n_slab)
    z_hi, inner = slab // 8, lax.rem(slab, 8)
    z_lo, x = pos // 4, lax.rem(pos, 4)
    cx, cy = labels.shape[1], labels.shape[2]

    local = [
        pltpu.make_async_copy(source, target, local_sem.at[i])
        for i, (source, target) in enumerate(
            (
                (load.at[0], d_x.at[pl.ds(1, 2), pl.ds(PAD, cx)]),
                (labels, label_x.at[pl.ds(1, 2)]),
                (potential.at[0], pot_x.at[pl.ds(1, 2), pl.ds(PAD, cx)]),
                (mask, mask_x),
            )
        )
    ]
    for copy in local:
        copy.start()

    offsets = [8 * o + i for o in (2, 1, 3) for i in range(8)] + list(range(1, 8))
    members = [{"slab": lax.rem(z_hi + c // 8, 4) * 8 + lax.rem(inner + c % 8, 8)} for c in offsets]

    def x_index(o):
        return lax.rem(x + o, 4)

    def z_index(o):
        return lax.rem(z_lo + o, 4)

    peers = list(members)
    peers += [{"pos": z_lo * 4 + x_index(o)} for o in range(1, 4)]
    peers += [{"pos": z_index(o) * 4 + x} for o in range(1, 4)]
    barrier = pltpu.get_barrier_semaphore()

    def greet(peer):
        pl.semaphore_signal(barrier, inc=1, device_id=peer, device_id_type=MESH)

    z_up, z_down = lax.rem(z_hi + 1, 4) * 8, lax.rem(z_hi + 3, 4) * 8
    is_first, is_last = inner == 0, inner == 7
    odd = lax.rem(inner, 2) == 1
    is_up_relay = jnp.logical_and(odd, inner < 7)
    is_down_relay = jnp.logical_and(jnp.logical_not(odd), inner > 0)
    for peer in peers:
        greet(peer)

    pl.semaphore_wait(barrier, len(peers))
    strip = cx // 4
    row = inner // 2

    def part(side, k):
        if k == 3 - 3 * side:
            return pl.ds(0 if side else 3 * strip, cx - 3 * strip)
        return pl.ds(k * strip + side * (cx - 4 * strip), strip)

    class Halo:
        def __init__(self, which, first, last, target, buffer):
            def send(source, where, peer, side, k):
                return pltpu.make_async_remote_copy(
                    src_ref=source,
                    dst_ref=where,
                    send_sem=send_sem.at[which, side, k],
                    recv_sem=recv_sem.at[which, side, k],
                    device_id={"slab": peer},
                    device_id_type=MESH,
                )

            def through(source, side, k, peer):
                return pltpu.make_async_remote_copy(
                    src_ref=source.at[part(side, k)],
                    dst_ref=buffer,
                    send_sem=send_sem.at[which, 2, k],
                    recv_sem=relay_recv.at[which],
                    device_id={"slab": peer},
                    device_id_type=MESH,
                )

            def forward(side, ghost, peer):
                first = row * strip + side * (cx - 4 * strip)
                where = pl.ds(pl.multiple_of(first, PAD), strip)
                return pltpu.make_async_remote_copy(
                    src_ref=buffer,
                    dst_ref=target(ghost).at[where],
                    send_sem=relay_send.at[which],
                    recv_sem=recv_sem.at[which, side, row],
                    device_id={"slab": peer},
                    device_id_type=MESH,
                )

            def pieces(source, side, ghost, peer):
                return [
                    send(
                        source.at[part(side, k)],
                        target(ghost).at[part(side, k)],
                        peer, side, k,
                    )
                    for k in range(4)
                ]

            self.whole = [
                (send(last, target(0), up, 0, 0), is_last, is_first),
                (send(first, target(3), down, 1, 0), is_first, is_last),
            ]
            self.parts = [pieces(last, 0, 0, up), pieces(first, 1, 3, down)]
            self.through = [
                [through(last, 0, k, z_hi * 8 + 2 * k + 1) for k in (0, 1, 2)],
                [through(first, 1, k, z_hi * 8 + 2 * k) for k in (1, 2, 3)],
            ]
            self.forward = [
                (is_up_relay, forward(0, 0, z_up)),
                (is_down_relay, forward(1, 3, z_down + 7)),
            ]
            self.arrive = through(last, 0, 0, z_hi * 8)

        def start(self):
            for side, (copy, leaves, _) in enumerate(self.whole):
                direct = self.parts[side][3 - 3 * side]

                @pl.when(leaves)
                def _():
                    for piece in self.through[side]:
                        piece.start()
                    direct.start()

                @pl.when(jnp.logical_not(leaves))
                def _():
                    copy.start()

        def relay(self):
            for role, copy in self.forward:

                @pl.when(role)
                def _():
                    self.arrive.wait_recv()
                    copy.start()

        def wait(self):
            for side, (copy, leaves, enters) in enumerate(self.whole):
                direct = self.parts[side][3 - 3 * side]

                @pl.when(enters)
                def _():
                    for piece in self.parts[side]:
                        piece.wait_recv()

                @pl.when(jnp.logical_not(enters))
                def _():
                    copy.wait_recv()

                @pl.when(leaves)
                def _():
                    for piece in self.through[side]:
                        piece.wait_send()
                    direct.wait_send()

                @pl.when(jnp.logical_not(leaves))
                def _():
                    copy.wait_send()

            for role, copy in self.forward:

                @pl.when(role)
                def _():
                    copy.wait_send()

    class Shared:
        def __init__(self, which, first, last, target):
            def send(source, where, peer, side):
                return pltpu.make_async_remote_copy(
                    src_ref=source,
                    dst_ref=where,
                    send_sem=send_sem.at[which, side, 0],
                    recv_sem=recv_sem.at[which, side, 0],
                    device_id={"slab": peer},
                    device_id_type=MESH,
                )

            quarter = pl.ds(pl.multiple_of(x * strip, strip), strip)

            def share(ghost, o):
                return pltpu.make_async_remote_copy(
                    src_ref=target(ghost).at[quarter],
                    dst_ref=target(ghost).at[quarter],
                    send_sem=share_send.at[o - 1],
                    recv_sem=share_recv.at[o - 1],
                    device_id={"pos": z_lo * 4 + x_index(o)},
                    device_id_type=MESH,
                )

            self.sides = [
                (
                    send(source, target(ghost), peer, side),
                    send(source.at[quarter], target(ghost).at[quarter], peer, side),
                    [share(ghost, o) for o in range(1, 4)],
                    leaves,
                    enters,
                )
                for side, (source, ghost, peer, leaves, enters) in enumerate(
                    ((last, 0, up, is_last, is_first), (first, 3, down, is_first, is_last))
                )
            ]

        def start(self):
            for whole, quarter, _, leaves, _ in self.sides:

                @pl.when(leaves)
                def _():
                    quarter.start()

                @pl.when(jnp.logical_not(leaves))
                def _():
                    whole.start()

        def relay(self):
            for _, quarter, shares, _, enters in self.sides:

                @pl.when(enters)
                def _():
                    quarter.wait_recv()
                    for share in shares:
                        share.start()

        def wait(self):
            for whole, quarter, shares, leaves, enters in self.sides:

                @pl.when(enters)
                def _():
                    for share in shares:
                        share.wait()

                @pl.when(jnp.logical_not(enters))
                def _():
                    whole.wait_recv()

                @pl.when(leaves)
                def _():
                    quarter.wait_send()

                @pl.when(jnp.logical_not(leaves))
                def _():
                    whole.wait_send()

    def padded(ref):
        return lambda layer: ref.at[layer, pl.ds(PAD, cx)]

    d_halo = Halo(0, load.at[0, 0], load.at[0, 1], padded(d_x), relay.at[0])
    label_halo = Shared(1, labels.at[0], labels.at[1], lambda layer: label_x.at[layer])
    pot_halo = Halo(2, potential.at[0, 0], potential.at[0, 1], padded(pot_x), relay.at[1])
    w_halo = Halo(3, padded(w_x)(1), padded(w_x)(2), padded(w_x), relay.at[2])
    label_halo.start()
    d_halo.start()

    for ref in (nu_x, d_x, w_x, pot_x):
        for layer in (1, 2):
            ref[layer, pl.ds(0, PAD), :] = jnp.zeros((PAD, cy), jnp.float32)
            ref[layer, pl.ds(PAD + cx, PAD), :] = jnp.zeros((PAD, cy), jnp.float32)

    low = jnp.where(slab > 0, 1.0, 0.0)
    high = jnp.where(slab < n_slab - 1, 1.0, 0.0)
    live = (low, 1.0, 1.0, high)
    table = [reluctivity[i] for i in range(4)]
    offset = shift[0]

    def materials(layers):
        def lookup(index):
            result = jnp.where(index == 1, table[1], table[0])
            result = jnp.where(index == 2, table[2], result)
            return jnp.where(index == 3, table[3], result)

        @pl.loop(0, cx // 2 // ROWS)
        def _(i):
            r = pl.multiple_of(i * ROWS, ROWS)
            s = pl.multiple_of(i * ROWS + cx // 2, ROWS)
            for layer in layers:
                turned = pltpu.roll(lookup(label_x[layer, pl.ds(r, ROWS), :]), offset, 1)
                nu_x[layer, pl.ds(PAD + r, ROWS), :] = turned * live[layer]
                still = lookup(label_x[layer, pl.ds(s, ROWS), :])
                nu_x[layer, pl.ds(PAD + s, ROWS), :] = still * live[layer]

    def at(ref, layer, r):
        return ref[layer, pl.ds(PAD + r, ROWS), :]

    def tall(ref, layer, r):
        return ref[layer, pl.ds(r, ROWS + 2 * PAD), :]

    def middle(block):
        return block[PAD : PAD + ROWS]

    def before(block):
        return pltpu.roll(block, 1, 0)

    def after(block):
        return pltpu.roll(block, ROWS + 2 * PAD - 1, 0)

    def operator(ref, layer, r, below, above):
        v_tall, nu_tall = tall(ref, layer, r), tall(nu_x, layer, r)
        flux = 0.5 * (nu_tall + after(nu_tall)) * (v_tall - after(v_tall))
        v, nu = middle(v_tall), middle(nu_tall)
        result = diagonal_shift * v + middle(flux - before(flux))
        for step, other in ((-1, below), (1, above)):
            if other is not None:
                result += 0.5 * (nu + at(nu_x, layer + step, r)) * (v - other)
        flux = 0.5 * (nu + pltpu.roll(nu, cy - 1, 1)) * (v - pltpu.roll(v, cy - 1, 1))
        return v, result + (flux - pltpu.roll(flux, 1, 1))

    zero = jnp.zeros((8, cy // 2), jnp.float32)

    local[1].wait()
    materials((1, 2))
    local[0].wait()

    @pl.loop(0, cx // ROWS)
    def _(i):
        r = pl.multiple_of(i * ROWS, ROWS)
        for layer, others in ((1, (None, at(d_x, 2, r))), (2, (at(d_x, 1, r), None))):
            _, image = operator(d_x, layer, r, *others)
            w_x[layer, pl.ds(PAD + r, ROWS), :] = image

    w_halo.start()
    pot_halo.start()
    label_halo.relay()
    d_halo.relay()
    w_halo.relay()
    pot_halo.relay()
    label_halo.wait()
    materials((0, 3))
    d_halo.wait()
    w_halo.wait()

    def sides(ref, layer, r):
        below, above = at(ref, layer - 1, r), at(ref, layer + 1, r)
        return (below * low, above) if layer == 1 else (below, above * high)

    def first_pass(i, sums):
        norm, energy = sums
        r = pl.multiple_of(i * ROWS, ROWS)
        for layer, ghost, exists in ((1, 0, low), (2, 3, high)):
            d = at(d_x, layer, r)
            nu = at(nu_x, layer, r) + at(nu_x, ghost, r)
            flux = 0.5 * nu * (d - at(d_x, ghost, r) * exists)
            image = at(w_x, layer, r) + flux
            w_x[layer, pl.ds(PAD + r, ROWS), :] = image
            w_x[ghost, pl.ds(PAD + r, ROWS), :] = at(w_x, ghost, r) - flux
            norm += fold(d * d)
            energy += fold(d * image)
        return norm, energy

    sums = lax.fori_loop(0, cx // ROWS, first_pass, (zero, zero))

    def whole_sum(part):
        return jnp.sum(jnp.sum(part, axis=0, keepdims=True), axis=1, keepdims=True)

    def wide(value, width=cy):
        return jnp.broadcast_to(value[:, :1], (1, width))

    def quotient(top, bottom):
        some = bottom > 0.0
        return jnp.where(some, top / jnp.where(some, bottom, 1.0), 0.0)

    norm, energy = [whole_sum(part) for part in sums]
    theta = quotient(energy, norm)
    theta_wide = wide(theta)
    def second_pass(i, sums):
        m1, m2, m3, m4 = sums
        r = pl.multiple_of(i * ROWS, ROWS)
        for layer in (1, 2):
            w, image = operator(w_x, layer, r, *sides(w_x, layer, r))
            d = at(d_x, layer, r)
            u = w - theta_wide * d
            q = image - theta_wide * w
            m1 += fold(d * u)
            m2 += fold(u * u)
            m3 += fold(u * q)
            m4 += fold(d * q)
        return m1, m2, m3, m4

    sums = lax.fori_loop(0, cx // ROWS, second_pass, (zero,) * 4)

    def combine():
        rows = box[:, 0, :]
        width = rows.shape[1]
        th, m0, m1, m2, m3, m4 = [pltpu.roll(rows, (width - i) % width, 1) for i in range(6)]
        total = lambda value: jnp.sum(value, axis=0, keepdims=True)
        centre = quotient(total(th * m0 + m1), total(m0))
        e = centre - th
        dw = m1 + th * m0
        return (
            centre,
            total(m0),
            total(m2 - e * (2.0 * m1 - e * m0)),
            total(m3 - e * (m2 + th * m1 + m4 - e * dw)),
        )

    def exchange(values):
        lane = lax.broadcasted_iota(jnp.int32, (1, tile.shape[1]), 1)
        packed = wide(values[0], tile.shape[1])
        for i, value in enumerate(values[1:], 1):
            packed = jnp.where(lane == i, wide(value, tile.shape[1]), packed)
        line = pl.ds(0, 1)
        tile[line, :] = packed
        copies = [
            pltpu.make_async_remote_copy(
                src_ref=tile.at[line],
                dst_ref=box.at[slab, line],
                send_sem=all_send.at[k],
                recv_sem=all_recv.at[k],
                device_id=peer,
                device_id_type=MESH,
            )
            for k, peer in enumerate(members)
        ]
        for copy in copies:
            copy.start()
        box[slab, line, :] = packed

        def finish():
            for copy in copies:
                copy.wait_recv()
            result = combine()
            return result, copies

        return finish

    values = (theta, norm, *[whole_sum(part) for part in sums])
    arrive = exchange(values)
    local[2].wait()
    local[3].wait()
    pot_halo.wait()

    def slopes(ref, layer, r):
        below, above = sides(ref, layer, r)
        v_tall = tall(ref, layer, r)
        v = middle(v_tall)
        return (
            above - below,
            middle(after(v_tall) - before(v_tall)),
            pltpu.roll(v, cy - 1, 1) - pltpu.roll(v, 1, 1),
        )

    @pl.loop(0, cx // ROWS)
    def _(i):
        r = pl.multiple_of(i * ROWS, ROWS)
        for layer in (1, 2):
            chosen = mask_x[layer - 1, pl.ds(r, ROWS), :].astype(jnp.float32)
            weight = 0.25 * chosen * at(nu_x, layer, r)
            pot = slopes(pot_x, layer, r)
            where = pl.ds((layer - 1) * cx + r, ROWS)
            for index, ref in enumerate((d_x, w_x)):
                other = slopes(ref, layer, r)
                fields[index, where, :] = weight * sum(p * q for p, q in zip(pot, other))
            fields[2, where, :] = 0.5 * weight * sum(p * p for p in pot)

    values, sent = arrive()
    centre, m0, m2, m3 = values
    alpha0 = 1.0 / centre
    beta = alpha0 * alpha0 * m2 / m0
    alpha1 = m2 / (m3 - alpha0 * m2 * (m2 / m0))
    from_d = wide(alpha0 + alpha1 * (1.0 + beta))
    from_w = wide(alpha0 * alpha1)

    def blend(rows):
        return from_d * fields[0, rows, :] - from_w * fields[1, rows, :] + fields[2, rows, :]

    quarter, small = 2 * cx // 4, 2 * cx // 16

    def x_peer(o):
        return {"pos": z_lo * 4 + x_index(o)}

    def z_peer(o):
        return {"pos": z_index(o) * 4 + x}

    def remote(source, target, send, recv, peer):
        return pltpu.make_async_remote_copy(
            src_ref=source, dst_ref=target, send_sem=send, recv_sem=recv, device_id=peer, device_id_type=MESH
        )

    def rows_of(index):
        return pl.ds(pl.multiple_of(index * small, small), small)

    order = (1, 2, 3, 0)
    along_x = {
        oz: [
            remote(
                term.at[rows_of(x_index(o) * 4 + z_index(oz))],
                part_x.at[o - 1, rows_of(z_index(oz))],
                x_send.at[0, oz, o - 1],
                x_recv.at[0, oz, o - 1],
                x_peer(o),
            )
            for o in range(1, 4)
        ]
        for oz in order
    }
    for oz in order:
        for o, copy in enumerate(along_x[oz], 1):
            rows = rows_of(x_index(o) * 4 + z_index(oz))
            term[rows, :] = blend(rows)
            copy.start()

    @pl.loop(0, cx // ROWS)
    def _(i):
        r = pl.multiple_of(i * ROWS, ROWS)
        for layer in (1, 2):
            value = from_d * at(d_x, layer, r) - from_w * at(w_x, layer, r)
            a_x[layer - 1, pl.ds(r, ROWS), :] = value

    finish = pltpu.make_async_copy(a_x, adjoint.at[0], out_sem.at[0])
    finish.start()
    for copy in sent:
        copy.wait_send()
    along_z = []
    for oz in order:
        for copy in along_x[oz]:
            copy.wait_recv()
        where = rows_of(z_index(oz))
        total = blend(rows_of(x * 4 + z_index(oz)))
        for o in range(3):
            total += part_x[o, where, :]
        piece[where, :] = total
        if oz:
            copy = remote(
                piece.at[where], part_z.at[oz - 1], z_send.at[0, oz - 1], z_recv.at[0, oz - 1], z_peer(oz)
            )
            copy.start()
            along_z.append(copy)
    for oz in order:
        for copy in along_x[oz]:
            copy.wait_send()
    for o, copy in enumerate(along_z):
        copy.wait()
        total += part_z[o]
    mine = rows_of(z_lo)
    merged[mine, :] = total / lax.axis_size("pos")

    def place(index):
        row = lax.rem(x, 2) * quarter + index * small
        return gradient.at[x // 2, pl.ds(pl.multiple_of(row, small), small)]

    gather_z = [
        remote(merged.at[mine], merged.at[mine], z_send.at[1, o - 1], z_recv.at[1, o - 1], z_peer(o))
        for o in range(1, 4)
    ]
    for copy in gather_z:
        copy.start()
    gather_x, keeps = [], []
    for oz in range(4):
        index = lax.rem(z_lo + 4 - oz, 4)
        if oz:
            gather_z[oz - 1].wait_recv()
        for o in range(1, 4):
            copy = remote(
                merged.at[rows_of(index)], place(index), x_send.at[1, oz, o - 1], x_recv.at[1, oz, o - 1], x_peer(o)
            )
            copy.start()
            gather_x.append(copy)
        keep = pltpu.make_async_copy(merged.at[rows_of(index)], place(index), out_sem.at[1 + oz])
        keep.start()
        keeps.append(keep)
    for copy in gather_x + keeps:
        copy.wait()
    for copy in gather_z:
        copy.wait_send()
    finish.wait()


def local(labels, magnet_mask, reluctivity, rotor_shift, potential, adjoint_load):
    cx, cy = labels.shape[1:]
    tall = cx + 2 * PAD
    floats = lambda *shape: pltpu.VMEM(shape, jnp.float32)
    sems = pltpu.SemaphoreType.DMA
    return pl.pallas_call(
        kernel,
        out_shape=(
            jax.ShapeDtypeStruct(labels.shape, jnp.float32),
            jax.ShapeDtypeStruct(adjoint_load.shape, jnp.float32),
        ),
        in_specs=[pl.BlockSpec(memory_space=pltpu.SMEM)] * 2 + [pl.BlockSpec(memory_space=pltpu.HBM)] * 4,
        out_specs=(pl.BlockSpec(memory_space=pl.ANY),) * 2,
        scratch_shapes=[
            pltpu.VMEM((4, cx, cy), jnp.int32),
            floats(4, tall, cy),
            floats(4, tall, cy),
            floats(4, tall, cy),
            floats(2, cx, cy),
            floats(4, tall, cy),
            pltpu.VMEM((2, cx, cy), jnp.int32),
            floats(2 * cx, cy),
            floats(3, 2 * cx, cy),
            floats(3, cx // 4, cy),
            floats(8, 128),
            floats(32, 8, 128),
            floats(3, cx // 2, cy),
            floats(3, cx // 8, cy),
            floats(cx // 2, cy),
            floats(cx // 2, cy),
            sems((4,)),
            sems((4, 3, 4)),
            sems((4, 2, 4)),
            sems((4,)),
            sems((4,)),
            sems((3,)),
            sems((3,)),
            sems((31,)),
            sems((31,)),
            sems((2, 4, 3)),
            sems((2, 4, 3)),
            sems((2, 3)),
            sems((2, 3)),
            sems((5,)),
        ],
        compiler_params=pltpu.CompilerParams(
            collective_id=0, has_side_effects=True, vmem_limit_bytes=24 << 20
        ),
    )(reluctivity, rotor_shift, *[pltpu.with_memory_space_constraint(v, pltpu.HBM) for v in (labels, magnet_mask, potential, adjoint_load)])


def solution(mesh):
    return jax.shard_map(
        local,
        mesh=mesh,
        in_specs=(
            P("slab", None, None),
            P("slab", None, None),
            P(),
            P("pos"),
            P("pos", "slab", None, None),
            P("pos", "slab", None, None),
        ),
        out_specs=(P("slab", None, None), P("pos", "slab", None, None)),
        check_vma=False,
    )
```
